512 devices in a mesh: frames: 32 (over z, core), phon: 4 (over y), chap: 4 (over x).
Axes of the slice: x: 4, y: 4, z: 16, core: 2. Of those that a mesh axis runs over, the one named last changes fastest.
Arguments:
- queries: bfloat16 [65536, 512], P(('chap', 'frames')), parts along dimension 0, may hold values from -80 to 80
- keys: bfloat16 [16384, 512], P(('chap', 'phon', 'frames')), parts along dimension 0, may hold values from -7 to 7
- values: bfloat16 [16384, 512], P(('chap', 'phon', 'frames')), parts along dimension 0, may hold values from -6 to 6
- band_first: int32 [128], P(('chap', 'frames')), parts along dimension 0, may hold values from 0 to 6, as said below
- cotangent: bfloat16 [65536, 512], P(('chap', 'frames')), parts along dimension 0, may hold values from -6 to 6
Outputs:
- aligned: bfloat16 [65536, 512], P(('chap', 'frames')), parts along dimension 0
- grad_query: bfloat16 [65536, 512], P(('chap', 'frames')), parts along dimension 0
- grad_key: float32 [16384, 512], P(('chap', 'phon', 'frames')), parts along dimension 0
- grad_value: float32 [16384, 512], P(('chap', 'phon', 'frames')), parts along dimension 0
The draws below stay inside these ranges and needn't reach their ends.
There are 4 independent parts, one for each index of `chap`. The reference program is written for one: setup_inputs(seed, part) draws one part's arguments, and reference() takes and returns one part's arrays. A program takes and returns all parts, laid end to end along the dimension named above; each array names one. Nothing has to cross between parts.
Inputs may be any that keep to these rules, and one draw needn't show every extreme that they name: Query tile i attends the key tiles band_first[i] to band_first[i] + 1.
All inputs are finite; a program needn't handle non-finite values.
Results may differ from the reference program's by a relative error of at most 0.022.
Values may be sent and summed in bfloat16 or wider, within the bound.
No kernel may reach another device: no remote copies, remote signals or barrier semaphores. Data moves between devices by JAX's collectives and lax.ppermute only.
A program may use at most 64 MiB of HBM per device.

```python
import jax
import jax.numpy as jnp
from jax import lax

D = 512
TILE = 512
NBAND = 2
FRAMES = 16384
PHONES = 4096
QT = 32
KT = 8


def band_plan(key):
    inner = jax.random.fold_in(key, 11)
    tiles = jnp.arange(QT, dtype=jnp.int32)
    base = tiles * (KT - NBAND) // (QT - 1)
    jitter = jax.random.randint(inner, (QT,), -1, 2).astype(jnp.int32)
    jitter = jnp.where((tiles == 0) | (tiles == QT - 1), 0, jitter)
    return jnp.clip(base + jitter, 0, KT - NBAND).astype(jnp.int32)


def key_table(key):
    inner = jax.random.fold_in(key, 23)
    table = jnp.clip(jax.random.normal(inner, (PHONES, D), jnp.float32), -6.0, 6.0)
    return table


def draw_band_first(key, part):
    return band_plan(key)


def draw_keys(key, part):
    return key_table(key).astype(jnp.bfloat16)


def draw_queries(key, part):
    inner = jax.random.fold_in(key, 41)
    base = jnp.clip(jax.random.normal(inner, (FRAMES, D), jnp.float32), -6.0, 6.0)
    return base.astype(jnp.bfloat16)


def levels(stream_key, shape, shards, smallest, top_value):
    def one(dim, parts):
        draws = jax.random.uniform(jax.random.fold_in(jax.random.fold_in(stream_key, 6), dim), (parts,), jnp.float32, smallest / len(shards), top_value / len(shards))
        return jnp.repeat(jnp.exp(draws), shape[dim] // parts).reshape((-1,) + (1,) * (len(shape) - dim - 1))

    level = one(*shards[0])
    for cut in shards[1:]:
        level = level * one(*cut)
    return level


def centred(stream_key, dims, spread, bound, cuts=(), kind=jnp.bfloat16):
    result = jax.random.normal(stream_key, dims, jnp.float32) * spread
    if len(cuts) > 0:
        result = levels(stream_key, dims, cuts, -0.22, 0.18) * result
    return jnp.clip(result, min=-bound, max=bound).astype(kind)


def setup_inputs(seed: int = 0, part: int = 0) -> dict:
    arg_keys = jax.random.split(jax.random.key(seed), 6)
    part_keys = jax.random.split(jax.random.fold_in(arg_keys[5], part), 6)
    return {
        "queries": draw_queries(jax.random.fold_in(jax.random.fold_in(arg_keys[5], part), 71), part),
        "keys": draw_keys(jax.random.fold_in(jax.random.fold_in(arg_keys[5], part), 71), part),
        "values": centred(part_keys[2], (PHONES, D), 1.0, 6.0, ((0, 128),)),
        "band_first": draw_band_first(jax.random.fold_in(jax.random.fold_in(arg_keys[5], part), 71), part),
        "cotangent": centred(part_keys[4], (FRAMES, D), 1.0, 6.0, ((0, 32),)),
    }


def tile_pass(q_tile, g_tile, first, keys, values):
    start = (first * TILE).astype(jnp.int32)
    k_band = lax.dynamic_slice_in_dim(keys, start, NBAND * TILE, 0)
    v_band = lax.dynamic_slice_in_dim(values, start, NBAND * TILE, 0)
    scale = D ** -0.5
    k_float = k_band.astype(jnp.float32)
    key_sq = jnp.sum(k_float * k_float, axis=1)
    scores = (jnp.dot(q_tile, k_band.T, preferred_element_type=jnp.float32) - 0.5 * key_sq[None, :]) * scale
    row_max = jnp.max(scores, axis=1, keepdims=True)
    expd = jnp.exp(scores - row_max)
    total = jnp.sum(expd, axis=1, keepdims=True)
    aligned_f = jnp.dot(expd.astype(jnp.bfloat16), v_band, preferred_element_type=jnp.float32) / total
    lse = row_max + jnp.log(total)
    probs = jnp.exp(scores - lse)
    d_probs = jnp.dot(g_tile, v_band.T, preferred_element_type=jnp.float32)
    delta = jnp.sum(g_tile.astype(jnp.float32) * aligned_f, axis=1, keepdims=True)
    d_scores = probs * (d_probs - delta)
    ds_low = d_scores.astype(jnp.bfloat16)
    grad_q = jnp.dot(ds_low, k_band, preferred_element_type=jnp.float32) * scale
    grad_k = (jnp.dot(ds_low.T, q_tile, preferred_element_type=jnp.float32) - jnp.sum(d_scores, axis=0)[:, None] * k_float) * scale
    grad_v = jnp.dot(probs.astype(jnp.bfloat16).T, g_tile, preferred_element_type=jnp.float32)
    return aligned_f.astype(jnp.bfloat16), grad_q.astype(jnp.bfloat16), grad_k, grad_v, start


def reference(queries, keys, values, band_first, cotangent):
    q_tiles = queries.reshape(QT, TILE, D)
    g_tiles = cotangent.reshape(QT, TILE, D)

    def step(carry, item):
        acc_key, acc_value = carry
        q_tile, g_tile, first = item
        out, grad_q, grad_k, grad_v, start = tile_pass(q_tile, g_tile, first, keys, values)
        old_key = lax.dynamic_slice_in_dim(acc_key, start, NBAND * TILE, 0)
        old_value = lax.dynamic_slice_in_dim(acc_value, start, NBAND * TILE, 0)
        acc_key = lax.dynamic_update_slice_in_dim(acc_key, old_key + grad_k, start, 0)
        acc_value = lax.dynamic_update_slice_in_dim(acc_value, old_value + grad_v, start, 0)
        return (acc_key, acc_value), (out, grad_q)

    init = (jnp.zeros((PHONES, D), jnp.float32), jnp.zeros((PHONES, D), jnp.float32))
    (grad_key, grad_value), (outs, grads) = lax.scan(step, init, (q_tiles, g_tiles, band_first))
    return outs.reshape(FRAMES, D), grads.reshape(FRAMES, D), grad_key, grad_value
```

```python
import jax
import jax.numpy as jnp
import numpy as np
from jax import lax
from jax.sharding import PartitionSpec as P

TILE = 512
NBAND = 2
NEG_FILL = -1e30
LIFT = 4096.0


def chip_order(offset):
    return [[(4 * g + (k + g) % 4 + offset) % 16 for g in range(4)] for k in range(4)]


ORDERS = [chip_order(0), chip_order(2)]
QUADS = [[2 * ORDERS[c][k][g] + c for k in range(4)] for c in range(2) for g in range(4)]
CROSSES = [[2 * ORDERS[c][k][g] + c for g in range(4)] for c in range(2) for k in range(4)]


def gathered(keys, values):
    both = jnp.concatenate([keys, values], axis=1).astype(jnp.float32) * LIFT
    every = lax.all_gather(both.astype(jnp.float16), "frames", axis=0, tiled=True)
    every = (every.astype(jnp.float32) * (1.0 / LIFT)).astype(jnp.bfloat16)
    width = keys.shape[1]
    return every[:, :width], every[:, width:]


def to_all_phon(value):
    n = lax.axis_size("phon")
    return lax.all_to_all(
        jnp.broadcast_to(value[None], (n, *value.shape)), "phon", 0, 0, tiled=True
    )


def shifted(value, axis, d):
    n = lax.axis_size(axis)
    return lax.ppermute(value, axis, [(i, (i + d) % n) for i in range(n)])


def f32_sum(parts):
    total = parts[0].astype(jnp.float32)
    for part in parts[1:]:
        total = total + part.astype(jnp.float32)
    return total


def body(queries, keys, values, band_first, cotangent):
    f32, bf16 = jnp.float32, jnp.bfloat16
    rows, width = queries.shape
    own = keys.shape[0]
    scale = width ** (-0.5)
    phon = lax.axis_index("phon")
    frame = lax.axis_index("frames")
    core = frame % 2
    block_keys, block_values = gathered(keys, values)
    block = block_keys.shape[0]
    key_tile = phon * (block // TILE) + jnp.arange(block, dtype=jnp.int32) // TILE
    allowed = (key_tile >= band_first[0]) & (key_tile < band_first[0] + NBAND)
    allowed = allowed[None, :]
    key_float = block_keys.astype(f32)
    key_sq = jnp.sum(key_float * key_float, axis=1)
    raw = (
        jnp.dot(queries, block_keys.T, preferred_element_type=f32) - 0.5 * key_sq[None, :]
    ) * scale
    scores = jnp.where(allowed, raw, NEG_FILL)
    local_max = jnp.max(scores, axis=1)
    expd = jnp.where(allowed, jnp.exp(scores - local_max[:, None]), 0.0)
    d_probs = jnp.dot(cotangent, block_values.T, preferred_element_type=f32)
    part_total = jnp.sum(expd, axis=1)
    part_delta = jnp.sum(expd * d_probs, axis=1)
    stats = to_all_phon(jnp.stack([local_max, part_total, part_delta]))
    row_max = jnp.max(stats[:, 0], axis=0)
    weight = jnp.exp(stats[:, 0] - row_max[None, :])
    total = jnp.sum(weight * stats[:, 1], axis=0)
    delta = jnp.sum(weight * stats[:, 2], axis=0) / total
    share = jnp.exp(local_max - row_max) / total
    probs = expd * share[:, None]
    probs_low = probs.astype(bf16)
    part_out = jnp.dot(probs_low, block_values, preferred_element_type=f32)
    d_scores = probs * (d_probs - delta[:, None])
    ds_low = d_scores.astype(bf16)
    part_query = jnp.dot(ds_low, block_keys, preferred_element_type=f32) * scale
    column_sum = jnp.sum(d_scores, axis=0)
    part_key = (
        jnp.einsum("qk,qd->kd", ds_low, queries, preferred_element_type=f32)
        - column_sum[:, None] * key_float
    ) * scale
    part_value = jnp.einsum("qk,qd->kd", probs_low, cotangent, preferred_element_type=f32)

    outs = jnp.concatenate([part_out.astype(bf16), part_query.astype(bf16)], axis=1)
    quarter = rows // 4
    outs = outs.reshape(4, quarter, 2 * width)
    pieces = [outs[phon]] + [shifted(outs[(phon + d) % 4], "phon", d) for d in (1, 3, 2)]

    grads = jnp.concatenate([part_key.astype(bf16), part_value.astype(bf16)], axis=1)
    grads = grads.reshape(block // own, own, 2 * width)
    table = jnp.asarray(np.asarray(ORDERS, np.int32).reshape(2, 16) * 2 + np.arange(2)[:, None], jnp.int32)
    keep = jnp.take(grads, table[core], axis=0)
    send = jnp.take(grads, table[1 - core], axis=0)
    n = lax.axis_size("frames")
    came = lax.ppermute(send, "frames", [(i, i ^ 1) for i in range(n)])
    first = f32_sum([keep, came]).astype(bf16).reshape(4, 4, own, 2 * width)
    first = lax.all_to_all(first, "frames", 0, 0, tiled=True, axis_index_groups=QUADS)
    mine = f32_sum(pieces).astype(bf16)
    spread = [mine] + [shifted(mine, "phon", d) for d in (1, 2, 3)]
    second = jnp.sum(first.astype(f32), axis=0).astype(bf16)
    second = lax.all_to_all(second, "frames", 0, 0, tiled=True, axis_index_groups=CROSSES)
    grad = jnp.sum(second.astype(f32), axis=0)
    everything = jnp.take(
        jnp.stack(spread), (phon - jnp.arange(4, dtype=jnp.int32)) % 4, axis=0
    ).reshape(rows, 2 * width)
    return (everything[:, :width], everything[:, width:], grad[:, :width], grad[:, width:])


def solution(mesh):
    in_specs = (
        P(("chap", "frames"), None),
        P(("chap", "phon", "frames"), None),
        P(("chap", "phon", "frames"), None),
        P(("chap", "frames")),
        P(("chap", "frames"), None),
    )
    out_specs = (
        P(("chap", "frames"), None),
        P(("chap", "frames"), None),
        P(("chap", "phon", "frames"), None),
        P(("chap", "phon", "frames"), None),
    )
    return jax.shard_map(body, mesh=mesh, in_specs=in_specs, out_specs=out_specs, check_vma=False)
```

```python
import jax
import jax.numpy as jnp
import numpy as np
from jax import lax
from jax.experimental import pallas as pl
from jax.experimental.pallas import tpu as pltpu
from jax.sharding import PartitionSpec as P


TILE = 512
NBAND = 2
NEG_FILL = -1e30
FLOOR = -1e29
LIFT = 4096.0
CHUNK = 128
NT = (((1,), (1,)), ((), ()))
F32, BF16 = jnp.float32, jnp.bfloat16


def chip_order(offset):
    return [[(4 * g + (k + g) % 4 + offset) % 16 for g in range(4)] for k in range(4)]


ORDERS = [chip_order(0), chip_order(2)]
QUADS = [[2 * ORDERS[c][k][g] + c for k in range(4)] for c in range(2) for g in range(4)]
CROSSES = [[2 * ORDERS[c][k][g] + c for g in range(4)] for c in range(2) for k in range(4)]
BLOCKS = [2 * ORDERS[c][k][g] + c for c in range(2) for k in range(4) for g in range(4)]


def vmem_call(kernel, out_shape, scalars, arrays, flops):
    spec = pl.BlockSpec(memory_space=pltpu.VMEM)
    size = sum(a.size * a.dtype.itemsize for a in arrays)
    size += sum(int(np.prod(o.shape)) * o.dtype.itemsize for o in out_shape)
    return pl.pallas_call(
        kernel,
        out_shape=out_shape,
        in_specs=[pl.BlockSpec(memory_space=pltpu.SMEM)] * len(scalars) + [spec] * len(arrays),
        out_specs=[spec] * len(out_shape),
        cost_estimate=pl.CostEstimate(flops=flops, bytes_accessed=size, transcendentals=0),
        compiler_params=pltpu.CompilerParams(vmem_limit_bytes=16 << 20),
    )(*scalars, *arrays)


def forward_kernel(flags, every, queries, cotangent, keys, values, expd, d_probs, stats):
    block, width = keys.shape
    own = block // len(BLOCKS)
    scale = width ** (-0.5)
    peak = jnp.full((1, queries.shape[0]), FLOOR, F32)
    for at in range(0, block, CHUNK):
        for i in range(at // own, (at + CHUNK) // own):
            piece = every[own * BLOCKS[i] : own * (BLOCKS[i] + 1), :]
            keys[own * i : own * (i + 1), :] = piece[:, :width]
            values[own * i : own * (i + 1), :] = piece[:, width:]
        here = slice(at, at + CHUNK)
        key = keys[here, :].astype(F32)
        offset = jnp.sum(key * key, axis=1, keepdims=True) * (-0.5 * scale)
        raw = lax.dot_general(keys[here, :], queries[...], NT, preferred_element_type=F32)
        scores = raw * scale + offset
        parts = [
            jnp.where(
                flags[own * BLOCKS[at // own + j] // TILE] > 0,
                scores[own * j : own * (j + 1)],
                NEG_FILL,
            )
            for j in range(CHUNK // own)
        ]
        scores = jnp.concatenate(parts, axis=0)
        expd[here, :] = scores
        peak = jnp.maximum(peak, jnp.max(scores, axis=0, keepdims=True))
    total = jnp.zeros_like(peak)
    delta = jnp.zeros_like(peak)
    for at in range(0, block, CHUNK):
        here = slice(at, at + CHUNK)
        e = jnp.exp(expd[here, :] - peak)
        expd[here, :] = e
        dp = lax.dot_general(values[here, :], cotangent[...], NT, preferred_element_type=F32)
        d_probs[here, :] = dp
        total += jnp.sum(e, axis=0, keepdims=True)
        delta += jnp.sum(e * dp, axis=0, keepdims=True)
    for i in range(stats.shape[0]):
        stats[i, 0:1, :] = peak
        stats[i, 1:2, :] = total
        stats[i, 2:3, :] = delta


def backward_kernel(
    start, stats, mine, expd, d_probs, keys, queries, cotangent, grads, probs_low, ds_low
):
    half, width = grads.shape[0], keys.shape[1]
    scale = width ** (-0.5)
    peaks = [stats[i, 0:1, :] for i in range(stats.shape[0])]
    peak = peaks[0]
    for p in peaks[1:]:
        peak = jnp.maximum(peak, p)
    total = jnp.zeros_like(peak)
    delta = jnp.zeros_like(peak)
    for i, p in enumerate(peaks):
        weight = jnp.exp(p - peak)
        total += weight * stats[i, 1:2, :]
        delta += weight * stats[i, 2:3, :]
    delta = delta / total
    share = jnp.exp(mine[0, 0:1, :] - peak) / total
    for at in range(0, half, CHUNK):
        there = pl.ds(pl.multiple_of(start[0] + at, CHUNK), CHUNK)
        here = slice(at, at + CHUNK)
        probs = expd[there, :] * share
        low = probs.astype(BF16)
        probs_low[here, :] = low
        value = jnp.dot(low, cotangent[...], preferred_element_type=F32)
        grads[here, width:] = value.astype(BF16)
        ds = probs * (d_probs[there, :] - delta)
        low = ds.astype(BF16)
        ds_low[here, :] = low
        column = jnp.sum(ds, axis=1, keepdims=True)
        key = jnp.dot(low, queries[...], preferred_element_type=F32)
        key = (key - column * keys[there, :].astype(F32)) * scale
        grads[here, :width] = key.astype(BF16)


def shifted(value, axis, d):
    n = lax.axis_size(axis)
    return lax.ppermute(value, axis, [(i, (i + d) % n) for i in range(n)])


def f32_sum(parts):
    total = parts[0].astype(F32)
    for part in parts[1:]:
        total = total + part.astype(F32)
    return total


def step(queries, keys, values, band_first, cotangent):
    rows, width = queries.shape
    own = keys.shape[0]
    scale = width ** (-0.5)
    phon = lax.axis_index("phon")
    core = lax.axis_index("frames") & 1
    n = lax.axis_size("frames")
    block = own * n
    half = block // 2
    tall = lambda dtype, r=block, w=width: jax.ShapeDtypeStruct((r, w), dtype)

    both = jnp.concatenate([keys, values], axis=1).astype(F32) * LIFT
    every = lax.all_gather(both.astype(jnp.float16), "frames", axis=0, tiled=True)
    every = (every.astype(F32) * (1.0 / LIFT)).astype(BF16)
    tiles = phon * (block // TILE) + jnp.arange(block // TILE, dtype=jnp.int32)
    flags = ((tiles >= band_first[0]) & (tiles < band_first[0] + NBAND)).astype(jnp.int32)
    work = 2 * block * rows * width
    block_keys, block_values, expd, d_probs, stats = vmem_call(
        forward_kernel,
        [tall(BF16), tall(BF16), tall(F32), tall(F32), jax.ShapeDtypeStruct((4, 3, rows), F32)],
        [flags],
        [every, queries, cotangent],
        2 * work,
    )
    all_stats = lax.all_to_all(stats, "phon", 0, 0, tiled=True)

    def backward(start):
        return vmem_call(
            backward_kernel,
            [tall(BF16, half, 2 * width), tall(BF16, half), tall(BF16, half)],
            [jnp.reshape(start, (1,)).astype(jnp.int32)],
            [all_stats, stats, expd, d_probs, block_keys, queries, cotangent],
            work,
        )

    send, send_probs, send_ds = backward((1 - core) * half)
    came = lax.ppermute(send, "frames", [(i, i ^ 1) for i in range(n)])
    keep, keep_probs, keep_ds = backward(core * half)
    first = f32_sum([keep, came]).astype(BF16).reshape(4, half // 4, 2 * width)
    first = lax.all_to_all(first, "frames", 0, 0, tiled=True, axis_index_groups=QUADS)

    def part(low_keep, low_send, right):
        one = lax.dynamic_slice_in_dim(right, core * half, half, axis=0)
        two = lax.dynamic_slice_in_dim(right, (1 - core) * half, half, axis=0)
        dims = (((0,), (0,)), ((), ()))
        return lax.dot_general(low_keep, one, dims, preferred_element_type=F32) + lax.dot_general(
            low_send, two, dims, preferred_element_type=F32
        )

    out = part(keep_probs, send_probs, block_values).astype(BF16)
    query = (part(keep_ds, send_ds, block_keys) * scale).astype(BF16)
    outs = jnp.concatenate([out, query], axis=1).reshape(4, rows // 4, 2 * width)
    pieces = [lax.dynamic_index_in_dim(outs, phon, 0, False)] + [
        shifted(lax.dynamic_index_in_dim(outs, (phon + d) & 3, 0, False), "phon", d)
        for d in (1, 2, 3)
    ]

    second = f32_sum([first[i] for i in range(4)]).astype(BF16).reshape(4, own, 2 * width)
    second, *pieces = lax.optimization_barrier((second, *pieces))
    mine = f32_sum(pieces).astype(BF16)
    second = lax.all_to_all(second, "frames", 0, 0, tiled=True, axis_index_groups=CROSSES)
    spread = [mine] + [shifted(mine, "phon", d) for d in (1, 2, 3)]
    everything = jnp.zeros((4, rows // 4, 2 * width), BF16)
    for d in range(4):
        everything = lax.dynamic_update_index_in_dim(everything, spread[d], (phon - d) & 3, 0)
    everything = everything.reshape(rows, 2 * width)
    grad = f32_sum([second[i] for i in range(4)])
    return (everything[:, :width], everything[:, width:], grad[:, :width], grad[:, width:])


def solution(mesh):
    in_specs = (
        P(("chap", "frames"), None),
        P(("chap", "phon", "frames"), None),
        P(("chap", "phon", "frames"), None),
        P(("chap", "frames")),
        P(("chap", "frames"), None),
    )
    out_specs = (
        P(("chap", "frames"), None),
        P(("chap", "frames"), None),
        P(("chap", "phon", "frames"), None),
        P(("chap", "phon", "frames"), None),
    )
    return jax.shard_map(step, mesh=mesh, in_specs=in_specs, out_specs=out_specs, check_vma=False)
```

```python
import jax
import jax.numpy as jnp
import numpy as np
from jax import lax
from jax.experimental import pallas as pl
from jax.experimental.pallas import tpu as pltpu
from jax.sharding import PartitionSpec as P


TILE = 512
NBAND = 2
NEG_FILL = -1e30
FLOOR = -1e29
LIFT = 4096.0
CHUNK = 128
NT = (((1,), (1,)), ((), ()))
TN = (((0,), (0,)), ((), ()))
F32, BF16 = jnp.float32, jnp.bfloat16


def chip_order(offset):
    return [[(4 * g + (k + g) % 4 + offset) % 16 for g in range(4)] for k in range(4)]


ORDERS = [chip_order(0), chip_order(2)]
QUADS = [[2 * ORDERS[c][k][g] + c for k in range(4)] for c in range(2) for g in range(4)]
CROSSES = [[2 * ORDERS[c][k][g] + c for g in range(4)] for c in range(2) for k in range(4)]
BLOCKS = [2 * ORDERS[c][k][g] + c for c in range(2) for k in range(4) for g in range(4)]


VMEM, HBM, SMEM = pltpu.VMEM, pltpu.HBM, pltpu.SMEM


def call(kernel, outs, args, scratch=(), flops=0):
    shapes = [
        HBM(shape, dtype) if space == HBM else jax.ShapeDtypeStruct(shape, dtype)
        for shape, dtype, space in outs
    ]
    size = sum(a.size * a.dtype.itemsize for a, _ in args)
    size += sum(int(np.prod(o.shape)) * o.dtype.itemsize for o in shapes)
    return pl.pallas_call(
        kernel,
        out_shape=shapes,
        in_specs=[pl.BlockSpec(memory_space=space) for _, space in args],
        out_specs=[pl.BlockSpec(memory_space=space) for _, _, space in outs],
        scratch_shapes=list(scratch),
        cost_estimate=pl.CostEstimate(flops=flops, bytes_accessed=size, transcendentals=0),
        compiler_params=pltpu.CompilerParams(vmem_limit_bytes=16 << 20),
    )(*[pltpu.with_memory_space_constraint(a, HBM) if space == HBM else a for a, space in args])


def pieces_of(x):
    hi = x.astype(BF16)
    rest = x - hi.astype(F32)
    mid = rest.astype(BF16)
    low = (rest - mid.astype(F32)).astype(BF16)
    return [hi, mid, low]


def joined(block, at):
    rows = [block[3 * at + j : 3 * at + j + 1, :].astype(F32) for j in range(3)]
    return rows[0] + (rows[1] + rows[2])


def masked(scores, flags, first, own):
    return jnp.concatenate(
        [
            jnp.where(flags[first + j] > 0, scores[own * j : own * (j + 1)], NEG_FILL)
            for j in range(scores.shape[0] // own)
        ],
        axis=0,
    )


def forward_kernel(
    flags, every, queries_far, cotangent_far, keys_far, values_far, parcel,
    scores_at, expd, keys, values, queries, cotangent, sems,
):
    block, width = keys.shape
    own = block // len(BLOCKS)
    scale = width ** (-0.5)
    rows = queries.shape[0]
    fetch_q = pltpu.make_async_copy(queries_far, queries, sems.at[0])
    fetch_g = pltpu.make_async_copy(cotangent_far, cotangent, sems.at[1])
    fetch_q.start()
    fetch_g.start()
    peak = jnp.full((1, rows), FLOOR, F32)
    for at in range(0, block, CHUNK):
        for i in range(at // own, (at + CHUNK) // own):
            piece = every[own * BLOCKS[i] : own * (BLOCKS[i] + 1), :]
            keys[own * i : own * (i + 1), :] = piece[:, :width]
            values[own * i : own * (i + 1), :] = piece[:, width:]
        if at == 0:
            fetch_q.wait()
        here = slice(at, at + CHUNK)
        key = keys[here, :].astype(F32)
        offset = jnp.sum(key * key, axis=1, keepdims=True) * (-0.5 * scale)
        raw = lax.dot_general(keys[here, :], queries[...], NT, preferred_element_type=F32)
        scores = masked(raw * scale + offset, flags, at // own, own)
        scores_at[here, :] = scores
        peak = jnp.maximum(peak, jnp.max(scores, axis=0, keepdims=True))
    store_k = pltpu.make_async_copy(keys, keys_far, sems.at[2])
    store_v = pltpu.make_async_copy(values, values_far, sems.at[3])
    store_k.start()
    store_v.start()
    total = jnp.zeros_like(peak)
    for at in range(0, block, CHUNK):
        here = slice(at, at + CHUNK)
        e = jnp.exp(scores_at[here, :] - peak)
        expd[here, :] = e.astype(BF16)
        total += jnp.sum(e, axis=0, keepdims=True)
    fetch_g.wait()
    ranks, deep = parcel.shape[0], parcel.shape[1]
    quarter = rows // ranks
    deltas = []
    for r in range(ranks):
        part = slice(quarter * r, quarter * (r + 1))
        out = lax.dot_general(expd[:, part], values[...], TN, preferred_element_type=F32)
        parcel[r, :quarter, :] = out.astype(BF16)
        delta = jnp.sum(cotangent[part, :].astype(F32) * out, axis=1, keepdims=True)
        deltas.append(jnp.transpose(jnp.broadcast_to(delta, (quarter, 128)))[0:1, :])
    delta = jnp.concatenate(deltas, axis=1)
    lines = pieces_of(peak) + pieces_of(total) + pieces_of(delta)
    lines += [jnp.zeros((1, rows), BF16)] * (deep - quarter - len(lines))
    lines = jnp.concatenate([x.astype(F32) for x in lines], axis=0).astype(BF16)
    for r in range(ranks):
        parcel[r, quarter:, :] = lines
    store_k.wait()
    store_v.wait()


def merged(blocks):
    peaks = [joined(b, 0) for b in blocks]
    peak = peaks[0]
    for p in peaks[1:]:
        peak = jnp.maximum(peak, p)
    weights = [jnp.exp(p - peak) for p in peaks]
    total = sum(w * joined(b, 1) for w, b in zip(weights, blocks))
    return peak, total, weights


def backward_kernel(
    start, flags, parcels, keys_far, values_far, queries_far, cotangent_far, grads, ds_far,
    keys, values, queries, cotangent, ds_low, sems, key_sems, value_sems, store_sems,
):
    half, width = keys.shape
    scale = width ** (-0.5)
    rows = queries.shape[0]
    own = 2 * half // len(BLOCKS)
    spots = range(0, half, CHUNK)
    there = [pl.ds(pl.multiple_of(start[0] + at, CHUNK), CHUNK) for at in spots]
    here = [pl.ds(at, CHUNK) for at in spots]
    fetch_q = pltpu.make_async_copy(queries_far, queries, sems.at[0])
    fetch_g = pltpu.make_async_copy(cotangent_far, cotangent, sems.at[1])
    fetch_k = [
        pltpu.make_async_copy(keys_far.at[t], keys.at[h], key_sems.at[i])
        for i, (t, h) in enumerate(zip(there, here))
    ]
    fetch_v = [
        pltpu.make_async_copy(values_far.at[t], values.at[h], value_sems.at[i])
        for i, (t, h) in enumerate(zip(there, here))
    ]
    fetch_k[0].start()
    fetch_q.start()
    fetch_g.start()
    fetch_v[0].start()
    for k, v in zip(fetch_k[1:], fetch_v[1:]):
        k.start()
        v.start()
    quarter = rows // parcels.shape[0]
    blocks = [parcels[i, quarter:, :] for i in range(parcels.shape[0])]
    peak, total, weights = merged(blocks)
    delta = sum(w * joined(b, 2) for w, b in zip(weights, blocks)) / total
    lse = peak + jnp.log(total)
    fetch_k[0].wait()
    fetch_q.wait()
    stores = []
    for i, spot in enumerate(here):
        if i > 0:
            fetch_k[i].wait()
        low_key = keys[spot, :]
        key = low_key.astype(F32)
        offset = jnp.sum(key * key, axis=1, keepdims=True) * (-0.5 * scale)
        raw = lax.dot_general(low_key, queries[...], NT, preferred_element_type=F32)
        scores = masked(raw * scale + offset, flags, start[0] // own + i * CHUNK // own, own)
        probs = jnp.exp(scores - lse)
        if i == 0:
            fetch_g.wait()
        value = jnp.dot(probs.astype(BF16), cotangent[...], preferred_element_type=F32)
        grads[spot, width:] = value.astype(BF16)
        fetch_v[i].wait()
        dp = lax.dot_general(values[spot, :], cotangent[...], NT, preferred_element_type=F32)
        ds = probs * (dp - delta)
        low = ds.astype(BF16)
        ds_low[spot, :] = low
        stores.append(pltpu.make_async_copy(ds_low.at[spot], ds_far.at[spot], store_sems.at[i]))
        stores[-1].start()
        column = jnp.sum(ds, axis=1, keepdims=True)
        grad = jnp.dot(low, queries[...], preferred_element_type=F32)
        grads[spot, :width] = ((grad - column * key) * scale).astype(BF16)
    for store in stores:
        store.wait()


def outputs_kernel(
    place, parcels, keys_far, keep_far, send_far, out, own_query, *rest
):
    moved, (keys, low, sems) = rest[:3], rest[3:]
    quarter, width = out.shape
    half = low.shape[1]
    phon, keep_at = place[0], place[1]
    fetch_k = pltpu.make_async_copy(keys_far, keys, sems.at[0])
    fetch_keep = pltpu.make_async_copy(keep_far, low.at[0], sems.at[1])
    fetch_send = pltpu.make_async_copy(send_far, low.at[1], sems.at[2])
    for f in (fetch_k, fetch_keep, fetch_send):
        f.start()
    mine = pl.ds(pl.multiple_of(phon * quarter, quarter), quarter)
    blocks = [parcels[i, quarter:, mine] for i in range(parcels.shape[0])]
    _, total, weights = merged(blocks)
    result = jnp.zeros((quarter, width), F32)
    for i, w in enumerate(weights):
        w = jnp.transpose(jnp.broadcast_to(w / total, (quarter, quarter)))
        w = jnp.concatenate([w] * (width // quarter), axis=1)
        result += w * parcels[i, :quarter, :].astype(F32)
    result = result.astype(BF16)
    out[...] = result
    for f in (fetch_k, fetch_keep, fetch_send):
        f.wait()
    for d in range(4):
        part = pl.ds(pl.multiple_of(((phon + d) & 3) * quarter, quarter), quarter)
        query = jnp.zeros((quarter, width), F32)
        for i, at in enumerate((keep_at, half - keep_at)):
            right = keys[pl.ds(pl.multiple_of(at, half), half), :]
            query += lax.dot_general(low[i, :, part], right, TN, preferred_element_type=F32)
        query = (query * width ** (-0.5)).astype(BF16)
        if d == 0:
            own_query[...] = query
        else:
            moved[d - 1][:, :width] = query
            moved[d - 1][:, width:] = result


def add_kernel(keep, came, out, made, sems):
    n = sems.shape[0]
    size = keep.shape[0] // n
    stores = []
    for i in range(n):
        part = pl.ds(size * i, size)
        made[part, :] = (keep[part, :].astype(F32) + came[part, :].astype(F32)).astype(BF16)
        stores.append(pltpu.make_async_copy(made.at[part], out.at[part], sems.at[i]))
        stores[-1].start()
    for store in stores:
        store.wait()


def sum_kernel(came, out):
    out[...] = f32_sum([came[j] for j in range(came.shape[0])]).astype(BF16)


def shifted(value, axis, d):
    n = lax.axis_size(axis)
    return lax.ppermute(value, axis, [(i, (i + d) % n) for i in range(n)])


def f32_sum(parts):
    total = parts[0].astype(F32)
    for part in parts[1:]:
        total = total + part.astype(F32)
    return total


def step(queries, keys, values, band_first, cotangent):
    rows, width = queries.shape
    own = keys.shape[0]
    phon = lax.axis_index("phon")
    core = lax.axis_index("frames") & 1
    n = lax.axis_size("frames")
    block = own * n
    half = block // 2
    ranks = lax.axis_size("phon")
    quarter = rows // ranks
    deep = quarter + 16
    dma = pltpu.SemaphoreType.DMA
    near = [pltpu.VMEM((rows, width), BF16)] * 2

    both = jnp.concatenate([keys, values], axis=1).astype(F32) * LIFT
    every = lax.all_gather(both.astype(jnp.float16), "frames", axis=0, tiled=True)
    every = (every.astype(F32) * (1.0 / LIFT)).astype(BF16)
    tiles = phon * (block // TILE) + jnp.asarray(np.asarray(BLOCKS, np.int32) * own // TILE)
    flags = ((tiles >= band_first[0]) & (tiles < band_first[0] + NBAND)).astype(jnp.int32)
    work = 2 * block * rows * width
    block_keys, block_values, parcel = call(
        forward_kernel,
        [((block, width), BF16, HBM)] * 2 + [((ranks, deep, width), BF16, VMEM)],
        [(flags, SMEM), (every, VMEM), (queries, HBM), (cotangent, HBM)],
        [
            pltpu.VMEM((block, rows), F32),
            pltpu.VMEM((block, rows), BF16),
            pltpu.VMEM((block, width), BF16),
            pltpu.VMEM((block, width), BF16),
            *near,
            dma((4,)),
        ],
        2 * work,
    )
    parcels = lax.all_to_all(parcel, "phon", 0, 0, tiled=True)

    def backward(start):
        return call(
            backward_kernel,
            [((half, 2 * width), BF16, VMEM), ((half, rows), BF16, HBM)],
            [
                (jnp.reshape(start, (1,)).astype(jnp.int32), SMEM),
                (flags, SMEM),
                (parcels, VMEM),
                (block_keys, HBM),
                (block_values, HBM),
                (queries, HBM),
                (cotangent, HBM),
            ],
            [pltpu.VMEM((half, width), BF16)] * 2
            + near
            + [pltpu.VMEM((half, rows), BF16), dma((2,))]
            + [dma((half // CHUNK,))] * 3,
            2 * work,
        )

    send, send_ds = backward((1 - core) * half)
    came = lax.ppermute(send, "frames", [(i, i ^ 1) for i in range(n)])
    keep, keep_ds = backward(core * half)
    (first,) = call(
        add_kernel,
        [((half, 2 * width), BF16, HBM)],
        [(keep, VMEM), (came, VMEM)],
        [pltpu.VMEM((half, 2 * width), BF16), dma((4,))],
    )
    first = lax.all_to_all(
        first.reshape(4, half // 4, 2 * width), "frames", 0, 0, tiled=True,
        axis_index_groups=QUADS,
    )

    place = jnp.stack([phon, core * half]).astype(jnp.int32)
    mine_out, own_query, *parts = call(
        outputs_kernel,
        [((quarter, width), BF16, VMEM)] * 2 + [((quarter, 2 * width), BF16, VMEM)] * 3,
        [
            (place, SMEM),
            (parcels, VMEM),
            (block_keys, HBM),
            (keep_ds, HBM),
            (send_ds, HBM),
        ],
        [pltpu.VMEM((block, width), BF16), pltpu.VMEM((2, half, rows), BF16), dma((3,))],
        work,
    )
    moved = [shifted(p, "phon", d) for d, p in zip((1, 2, 3), parts)]

    (second,) = call(sum_kernel, [((half // 4, 2 * width), BF16, VMEM)], [(first, VMEM)])
    second = lax.all_to_all(
        second.reshape(4, own, 2 * width), "frames", 0, 0, tiled=True,
        axis_index_groups=CROSSES,
    )
    mine_query = f32_sum([own_query] + [m[:, :width] for m in moved]).astype(BF16)
    spread = [mine_query] + [shifted(mine_query, "phon", d) for d in (1, 2, 3)]

    def placed(parts):
        whole = jnp.zeros((ranks, quarter, width), BF16)
        for d, p in enumerate(parts):
            whole = lax.dynamic_update_index_in_dim(whole, p, (phon - d) & 3, 0)
        return whole.reshape(rows, width)

    aligned = placed([mine_out] + [m[:, width:] for m in moved])
    grad_query = placed(spread)
    grad = f32_sum([second[i] for i in range(4)])
    return (aligned, grad_query, grad[:, :width], grad[:, width:])


def solution(mesh):
    in_specs = (
        P(("chap", "frames"), None),
        P(("chap", "phon", "frames"), None),
        P(("chap", "phon", "frames"), None),
        P(("chap", "frames")),
        P(("chap", "frames"), None),
    )
    out_specs = (
        P(("chap", "frames"), None),
        P(("chap", "frames"), None),
        P(("chap", "phon", "frames"), None),
        P(("chap", "phon", "frames"), None),
    )
    return jax.shard_map(step, mesh=mesh, in_specs=in_specs, out_specs=out_specs, check_vma=False)
```

```python
import jax
import jax.numpy as jnp
import numpy as np
from jax import lax
from jax.experimental import pallas as pl
from jax.experimental.pallas import tpu as pltpu
from jax.sharding import PartitionSpec as P


TILE = 512
NBAND = 2
NEG_FILL = -1e30
FLOOR = -1e29
LIFT = 4096.0
CHUNK = 512
NT = (((1,), (1,)), ((), ()))
TN = (((0,), (0,)), ((), ()))
F32, BF16 = jnp.float32, jnp.bfloat16


def chip_order(offset):
    return [[(4 * g + (k + g) % 4 + offset) % 16 for g in range(4)] for k in range(4)]


ORDERS = [chip_order(0), chip_order(2)]
QUADS = [[2 * ORDERS[c][k][g] + c for k in range(4)] for c in range(2) for g in range(4)]
CROSSES = [[2 * ORDERS[c][k][g] + c for g in range(4)] for c in range(2) for k in range(4)]
BLOCKS = [2 * ORDERS[c][k][g] + c for c in range(2) for k in range(4) for g in range(4)]


VMEM, HBM, SMEM = pltpu.VMEM, pltpu.HBM, pltpu.SMEM


def call(kernel, outs, args, scratch=(), flops=0):
    shapes = [
        HBM(shape, dtype) if space == HBM else jax.ShapeDtypeStruct(shape, dtype)
        for shape, dtype, space in outs
    ]
    size = sum(a.size * a.dtype.itemsize for a, _ in args)
    size += sum(int(np.prod(o.shape)) * o.dtype.itemsize for o in shapes)
    return pl.pallas_call(
        kernel,
        out_shape=shapes,
        in_specs=[pl.BlockSpec(memory_space=space) for _, space in args],
        out_specs=[pl.BlockSpec(memory_space=space) for _, _, space in outs],
        scratch_shapes=list(scratch),
        cost_estimate=pl.CostEstimate(flops=flops, bytes_accessed=size, transcendentals=0),
        compiler_params=pltpu.CompilerParams(vmem_limit_bytes=16 << 20),
    )(*[pltpu.with_memory_space_constraint(a, HBM) if space == HBM else a for a, space in args])


def masked(scores, flags, first, own):
    return jnp.concatenate(
        [
            jnp.where(flags[first + j] > 0, scores[own * j : own * (j + 1)], NEG_FILL)
            for j in range(scores.shape[0] // own)
        ],
        axis=0,
    )


def forward_kernel(
    flags, every, queries_far, cotangent_far, keys_far, values_far, features_far, stats,
    scores_at, expd, keys, values, queries, cotangent, features, sems,
):
    block, width = keys.shape
    own = block // len(BLOCKS)
    scale = width ** (-0.5)
    rows = queries.shape[0]
    fetch_q = pltpu.make_async_copy(queries_far, queries, sems.at[0])
    fetch_g = pltpu.make_async_copy(cotangent_far, cotangent, sems.at[1])
    fetch_q.start()
    fetch_g.start()
    peak = jnp.full((1, rows), FLOOR, F32)
    for at in range(0, block, CHUNK):
        for i in range(at // own, (at + CHUNK) // own):
            piece = every[own * BLOCKS[i] : own * (BLOCKS[i] + 1), :]
            keys[own * i : own * (i + 1), :] = piece[:, :width]
            values[own * i : own * (i + 1), :] = piece[:, width:]
        if at == 0:
            fetch_q.wait()
        here = slice(at, at + CHUNK)
        key = keys[here, :].astype(F32)
        offset = jnp.sum(key * key, axis=1, keepdims=True) * (-0.5 * scale)
        raw = lax.dot_general(keys[here, :], queries[...], NT, preferred_element_type=F32)
        scores = masked(raw * scale + offset, flags, at // own, own)
        scores_at[here, :] = scores
        peak = jnp.maximum(peak, jnp.max(scores, axis=0, keepdims=True))
    store_k = pltpu.make_async_copy(keys, keys_far, sems.at[2])
    store_v = pltpu.make_async_copy(values, values_far, sems.at[3])
    store_k.start()
    store_v.start()
    total = jnp.zeros_like(peak)
    for at in range(0, block, CHUNK):
        here = slice(at, at + CHUNK)
        e = jnp.exp(scores_at[here, :] - peak)
        expd[here, :] = e.astype(BF16)
        total += jnp.sum(e, axis=0, keepdims=True)
    out = lax.dot_general(expd[...], values[...], TN, preferred_element_type=F32)
    features[...] = out.astype(BF16)
    store_f = pltpu.make_async_copy(features, features_far, sems.at[4])
    store_f.start()
    fetch_g.wait()
    delta = jnp.sum(cotangent[...].astype(F32) * out, axis=1, keepdims=True)
    delta = jnp.transpose(jnp.broadcast_to(delta, (rows, 128)))[0:1, :]
    for r in range(stats.shape[0]):
        stats[r, 0:1, :] = peak
        stats[r, 1:2, :] = total
        stats[r, 2:3, :] = delta
    store_k.wait()
    store_v.wait()
    store_f.wait()


def merged(stats):
    peaks = [stats[i, 0:1, :] for i in range(stats.shape[0])]
    peak = peaks[0]
    for p in peaks[1:]:
        peak = jnp.maximum(peak, p)
    weights = [jnp.exp(p - peak) for p in peaks]
    total = sum(w * stats[i, 1:2, :] for i, w in enumerate(weights))
    delta = sum(w * stats[i, 2:3, :] for i, w in enumerate(weights))
    return peak, total, delta


def backward_kernel(
    start, flags, stats, keys_far, values_far, queries_far, cotangent_far, grads, ds_far,
    keys, values, queries, cotangent, ds_low, sems, key_sems, value_sems, store_sems,
):
    half, width = keys.shape
    scale = width ** (-0.5)
    own = 2 * half // len(BLOCKS)
    spots = range(0, half, CHUNK)
    there = [pl.ds(pl.multiple_of(start[0] + at, CHUNK), CHUNK) for at in spots]
    here = [pl.ds(at, CHUNK) for at in spots]
    fetch_q = pltpu.make_async_copy(queries_far, queries, sems.at[0])
    fetch_g = pltpu.make_async_copy(cotangent_far, cotangent, sems.at[1])
    fetch_k = [
        pltpu.make_async_copy(keys_far.at[t], keys.at[h], key_sems.at[i])
        for i, (t, h) in enumerate(zip(there, here))
    ]
    fetch_v = [
        pltpu.make_async_copy(values_far.at[t], values.at[h], value_sems.at[i])
        for i, (t, h) in enumerate(zip(there, here))
    ]
    fetch_k[0].start()
    fetch_q.start()
    fetch_g.start()
    fetch_v[0].start()
    for k, v in zip(fetch_k[1:], fetch_v[1:]):
        k.start()
        v.start()
    peak, total, delta = merged(stats)
    delta = delta / total
    lse = peak + jnp.log(total)
    fetch_k[0].wait()
    fetch_q.wait()
    stores = []
    for i, spot in enumerate(here):
        if i > 0:
            fetch_k[i].wait()
        low_key = keys[spot, :]
        key = low_key.astype(F32)
        offset = jnp.sum(key * key, axis=1, keepdims=True) * (-0.5 * scale)
        raw = lax.dot_general(low_key, queries[...], NT, preferred_element_type=F32)
        scores = masked(raw * scale + offset, flags, start[0] // own + i * CHUNK // own, own)
        probs = jnp.exp(scores - lse)
        if i == 0:
            fetch_g.wait()
        value = jnp.dot(probs.astype(BF16), cotangent[...], preferred_element_type=F32)
        grads[spot, width:] = value.astype(BF16)
        fetch_v[i].wait()
        dp = lax.dot_general(values[spot, :], cotangent[...], NT, preferred_element_type=F32)
        ds = probs * (dp - delta)
        low = ds.astype(BF16)
        ds_low[spot, :] = low
        stores.append(pltpu.make_async_copy(ds_low.at[spot], ds_far.at[spot], store_sems.at[i]))
        stores[-1].start()
        column = jnp.sum(ds, axis=1, keepdims=True)
        grad = jnp.dot(low, queries[...], preferred_element_type=F32)
        grads[spot, :width] = ((grad - column * key) * scale).astype(BF16)
    for store in stores:
        store.wait()


def outputs_kernel(
    place, stats, own_stats, keys_far, features_far, keep_far, send_far, *rest
):
    parts, (keys, features, low, gathered, sems) = rest[:4], rest[4:]
    quarter = parts[0].shape[0]
    half, rows = low.shape[1:]
    width = keys.shape[1]
    fetches = [
        pltpu.make_async_copy(far, near, sems.at[i])
        for i, (far, near) in enumerate(
            ((keep_far, low.at[0]), (send_far, low.at[1]), (keys_far, keys),
             (features_far, features))
        )
    ]
    for f in fetches:
        f.start()
    peak, total, _ = merged(stats)
    share = jnp.exp(own_stats[0, 0:1, :] - peak) / total
    for f in fetches[:3]:
        f.wait()
    query = jnp.zeros((rows, width), F32)
    for i, at in enumerate((place[1], half - place[1])):
        right = keys[pl.ds(pl.multiple_of(at, half), half), :]
        query += lax.dot_general(low[i], right, TN, preferred_element_type=F32)
    gathered[:, :width] = (query * width ** (-0.5)).astype(BF16)
    fetches[3].wait()
    share = jnp.transpose(jnp.broadcast_to(share, (128, rows)))
    share = jnp.concatenate([share] * (width // 128), axis=1)
    gathered[:, width:] = (features[...].astype(F32) * share).astype(BF16)
    for d, part in enumerate(parts):
        at = ((place[0] + d) & 3) * quarter
        part[...] = gathered[pl.ds(pl.multiple_of(at, quarter), quarter), :]


def add_kernel(keep, came, out, made, sems):
    n = sems.shape[0]
    size = keep.shape[0] // n
    stores = []
    for i in range(n):
        part = pl.ds(size * i, size)
        made[part, :] = (keep[part, :].astype(F32) + came[part, :].astype(F32)).astype(BF16)
        stores.append(pltpu.make_async_copy(made.at[part], out.at[part], sems.at[i]))
        stores[-1].start()
    for store in stores:
        store.wait()


def sum_kernel(came, out):
    out[...] = f32_sum([came[j] for j in range(came.shape[0])]).astype(BF16)


def shifted(value, axis, d):
    n = lax.axis_size(axis)
    return lax.ppermute(value, axis, [(i, (i + d) % n) for i in range(n)])


def f32_sum(parts):
    total = parts[0].astype(F32)
    for part in parts[1:]:
        total = total + part.astype(F32)
    return total


def step(queries, keys, values, band_first, cotangent):
    rows, width = queries.shape
    own = keys.shape[0]
    phon = lax.axis_index("phon")
    core = lax.axis_index("frames") & 1
    n = lax.axis_size("frames")
    block = own * n
    half = block // 2
    ranks = lax.axis_size("phon")
    quarter = rows // ranks
    dma = pltpu.SemaphoreType.DMA
    near = [pltpu.VMEM((rows, width), BF16)] * 2

    both = jnp.concatenate([keys, values], axis=1).astype(F32) * LIFT
    every = lax.all_gather(both.astype(jnp.float16), "frames", axis=0, tiled=True)
    every = (every.astype(F32) * (1.0 / LIFT)).astype(BF16)
    tiles = phon * (block // TILE) + jnp.asarray(np.asarray(BLOCKS, np.int32) * own // TILE)
    flags = ((tiles >= band_first[0]) & (tiles < band_first[0] + NBAND)).astype(jnp.int32)
    work = 2 * block * rows * width
    block_keys, block_values, features, stats = call(
        forward_kernel,
        [((block, width), BF16, HBM)] * 2
        + [((rows, width), BF16, HBM), ((ranks, 3, rows), F32, VMEM)],
        [(flags, SMEM), (every, VMEM), (queries, HBM), (cotangent, HBM)],
        [
            pltpu.VMEM((block, rows), F32),
            pltpu.VMEM((block, rows), BF16),
            pltpu.VMEM((block, width), BF16),
            pltpu.VMEM((block, width), BF16),
            *near,
            pltpu.VMEM((rows, width), BF16),
            dma((5,)),
        ],
        2 * work,
    )
    all_stats = lax.all_to_all(stats, "phon", 0, 0, tiled=True)

    def backward(start):
        return call(
            backward_kernel,
            [((half, 2 * width), BF16, VMEM), ((half, rows), BF16, HBM)],
            [
                (jnp.reshape(start, (1,)).astype(jnp.int32), SMEM),
                (flags, SMEM),
                (all_stats, VMEM),
                (block_keys, HBM),
                (block_values, HBM),
                (queries, HBM),
                (cotangent, HBM),
            ],
            [pltpu.VMEM((half, width), BF16)] * 2
            + near
            + [pltpu.VMEM((half, rows), BF16), dma((2,))]
            + [dma((half // CHUNK,))] * 3,
            2 * work,
        )

    send, send_ds = backward((1 - core) * half)
    came = lax.ppermute(send, "frames", [(i, i ^ 1) for i in range(n)])
    keep, keep_ds = backward(core * half)
    (first,) = call(
        add_kernel,
        [((half, 2 * width), BF16, HBM)],
        [(keep, VMEM), (came, VMEM)],
        [pltpu.VMEM((half, 2 * width), BF16), dma((4,))],
    )
    first = lax.all_to_all(
        first.reshape(4, half // 4, 2 * width), "frames", 0, 0, tiled=True,
        axis_index_groups=QUADS,
    )

    place = jnp.stack([phon, core * half]).astype(jnp.int32)
    parts = call(
        outputs_kernel,
        [((quarter, 2 * width), BF16, VMEM)] * 4,
        [
            (place, SMEM),
            (all_stats, VMEM),
            (stats, VMEM),
            (block_keys, HBM),
            (features, HBM),
            (keep_ds, HBM),
            (send_ds, HBM),
        ],
        [
            pltpu.VMEM((block, width), BF16),
            pltpu.VMEM((rows, width), BF16),
            pltpu.VMEM((2, half, rows), BF16),
            pltpu.VMEM((rows, 2 * width), BF16),
            dma((4,)),
        ],
        work,
    )
    moved = [parts[0]] + [shifted(p, "phon", d) for d, p in enumerate(parts) if d > 0]

    (second,) = call(sum_kernel, [((half // 4, 2 * width), BF16, VMEM)], [(first, VMEM)])
    second = lax.all_to_all(
        second.reshape(4, own, 2 * width), "frames", 0, 0, tiled=True,
        axis_index_groups=CROSSES,
    )
    mine = f32_sum(moved).astype(BF16)
    spread = [mine] + [shifted(mine, "phon", d) for d in (1, 2, 3)]

    def placed(parts):
        whole = jnp.zeros((ranks, quarter, width), BF16)
        for d, p in enumerate(parts):
            whole = lax.dynamic_update_index_in_dim(whole, p, (phon - d) & 3, 0)
        return whole.reshape(rows, width)

    grad_query = placed([m[:, :width] for m in spread])
    aligned = placed([m[:, width:] for m in spread])
    grad = f32_sum([second[i] for i in range(4)])
    return (aligned, grad_query, grad[:, :width], grad[:, width:])


def solution(mesh):
    in_specs = (
        P(("chap", "frames"), None),
        P(("chap", "phon", "frames"), None),
        P(("chap", "phon", "frames"), None),
        P(("chap", "frames")),
        P(("chap", "frames"), None),
    )
    out_specs = (
        P(("chap", "frames"), None),
        P(("chap", "frames"), None),
        P(("chap", "phon", "frames"), None),
        P(("chap", "phon", "frames"), None),
    )
    return jax.shard_map(step, mesh=mesh, in_specs=in_specs, out_specs=out_specs, check_vma=False)
```

```python
import jax
import jax.numpy as jnp
import numpy as np
from jax import lax
from jax.experimental import pallas as pl
from jax.experimental.pallas import tpu as pltpu
from jax.sharding import PartitionSpec as P


TILE = 512
NBAND = 2
NEG_FILL = -1e30
FLOOR = -1e29
LIFT = 4096.0
CHUNK = 512
NT = (((1,), (1,)), ((), ()))
TN = (((0,), (0,)), ((), ()))
F32, BF16 = jnp.float32, jnp.bfloat16


def chip_order(offset):
    return [[(4 * g + (k + g) % 4 + offset) % 16 for g in range(4)] for k in range(4)]


ORDERS = [chip_order(0), chip_order(2)]
QUADS = [[2 * ORDERS[c][k][g] + c for k in range(4)] for c in range(2) for g in range(4)]
CROSSES = [[2 * ORDERS[c][k][g] + c for g in range(4)] for c in range(2) for k in range(4)]
BLOCKS = [2 * ORDERS[c][k][g] + c for c in range(2) for k in range(4) for g in range(4)]


VMEM, HBM, SMEM = pltpu.VMEM, pltpu.HBM, pltpu.SMEM


def call(kernel, outs, args, scratch=(), flops=0):
    shapes = [
        HBM(shape, dtype) if space == HBM else jax.ShapeDtypeStruct(shape, dtype)
        for shape, dtype, space in outs
    ]
    size = sum(a.size * a.dtype.itemsize for a, _ in args)
    size += sum(int(np.prod(o.shape)) * o.dtype.itemsize for o in shapes)
    return pl.pallas_call(
        kernel,
        out_shape=shapes,
        in_specs=[pl.BlockSpec(memory_space=space) for _, space in args],
        out_specs=[pl.BlockSpec(memory_space=space) for _, _, space in outs],
        scratch_shapes=list(scratch),
        cost_estimate=pl.CostEstimate(flops=flops, bytes_accessed=size, transcendentals=0),
        compiler_params=pltpu.CompilerParams(vmem_limit_bytes=16 << 20),
    )(*[pltpu.with_memory_space_constraint(a, HBM) if space == HBM else a for a, space in args])


def masked(scores, flags, first, own):
    return jnp.concatenate(
        [
            jnp.where(flags[first + j] > 0, scores[own * j : own * (j + 1)], NEG_FILL)
            for j in range(scores.shape[0] // own)
        ],
        axis=0,
    )


def forward_kernel(
    flags, every, queries_far, cotangent_far, keys, values, features_far, stats,
    scores_at, expd, queries, cotangent, features, sems,
):
    block, width = keys.shape
    own = block // len(BLOCKS)
    scale = width ** (-0.5)
    rows = queries.shape[0]
    fetch_q = pltpu.make_async_copy(queries_far, queries, sems.at[0])
    fetch_g = pltpu.make_async_copy(cotangent_far, cotangent, sems.at[1])
    fetch_q.start()
    fetch_g.start()
    peak = jnp.full((1, rows), FLOOR, F32)
    for at in range(0, block, CHUNK):
        for i in range(at // own, (at + CHUNK) // own):
            piece = every[own * BLOCKS[i] : own * (BLOCKS[i] + 1), :]
            keys[own * i : own * (i + 1), :] = piece[:, :width]
            values[own * i : own * (i + 1), :] = piece[:, width:]
        if at == 0:
            fetch_q.wait()
        here = slice(at, at + CHUNK)
        key = keys[here, :].astype(F32)
        offset = jnp.sum(key * key, axis=1, keepdims=True) * (-0.5 * scale)
        raw = lax.dot_general(keys[here, :], queries[...], NT, preferred_element_type=F32)
        scores = masked(raw * scale + offset, flags, at // own, own)
        scores_at[here, :] = scores
        peak = jnp.maximum(peak, jnp.max(scores, axis=0, keepdims=True))
    total = jnp.zeros_like(peak)
    for at in range(0, block, CHUNK):
        here = slice(at, at + CHUNK)
        e = jnp.exp(scores_at[here, :] - peak)
        expd[here, :] = e.astype(BF16)
        total += jnp.sum(e, axis=0, keepdims=True)
    out = lax.dot_general(expd[...], values[...], TN, preferred_element_type=F32)
    features[...] = out.astype(BF16)
    store_f = pltpu.make_async_copy(features, features_far, sems.at[2])
    store_f.start()
    fetch_g.wait()
    delta = jnp.sum(cotangent[...].astype(F32) * out, axis=1, keepdims=True)
    delta = jnp.transpose(jnp.broadcast_to(delta, (rows, 128)))[0:1, :]
    stats[0:1, :] = peak
    stats[1:2, :] = total
    stats[2:3, :] = delta
    store_f.wait()


def merged(heard):
    peaks = [stats[0:1, :] for stats in heard]
    peak = peaks[0]
    for p in peaks[1:]:
        peak = jnp.maximum(peak, p)
    weights = [jnp.exp(p - peak) for p in peaks]
    total = sum(w * stats[1:2, :] for w, stats in zip(weights, heard))
    delta = sum(w * stats[2:3, :] for w, stats in zip(weights, heard))
    return peak, jnp.maximum(total, 0.5), delta


def backward_kernel(
    start, flags, stats, stats_up, stats_down, keys, values, queries_far, cotangent_far,
    grads_out, ds_far, queries, cotangent, grads, ds_low, sems,
):
    half, width = grads.shape[0], keys.shape[1]
    scale = width ** (-0.5)
    own = 2 * half // len(BLOCKS)
    mine = pl.ds(pl.multiple_of(start[0], half), half)
    fetch_q = pltpu.make_async_copy(queries_far, queries, sems.at[0])
    fetch_g = pltpu.make_async_copy(cotangent_far, cotangent, sems.at[1])
    fetch_q.start()
    fetch_g.start()
    peak, total, delta = merged((stats, stats_up, stats_down))
    delta = delta / total
    lse = peak + jnp.log(total)
    low_key = keys[mine, :]
    key = low_key.astype(F32)
    offset = jnp.sum(key * key, axis=1, keepdims=True) * (-0.5 * scale)
    fetch_q.wait()
    raw = lax.dot_general(low_key, queries[...], NT, preferred_element_type=F32)
    fetch_g.wait()
    dp = lax.dot_general(values[mine, :], cotangent[...], NT, preferred_element_type=F32)
    scores = masked(raw * scale + offset, flags, start[0] // own, own)
    probs = jnp.exp(scores - lse)
    value = jnp.dot(probs.astype(BF16), cotangent[...], preferred_element_type=F32)
    grads[:, width:] = value.astype(BF16)
    right = pl.ds(width, width)
    store_value = pltpu.make_async_copy(grads.at[:, right], grads_out.at[:, right], sems.at[4])
    store_value.start()
    ds = probs * (dp - delta)
    low = ds.astype(BF16)
    ds_low[...] = low
    store_ds = pltpu.make_async_copy(ds_low, ds_far, sems.at[2])
    store_ds.start()
    column = jnp.sum(ds, axis=1, keepdims=True)
    grad = jnp.dot(low, queries[...], preferred_element_type=F32)
    grads[:, :width] = ((grad - column * keys[mine, :].astype(F32)) * scale).astype(BF16)
    left = pl.ds(0, width)
    store_key = pltpu.make_async_copy(grads.at[:, left], grads_out.at[:, left], sems.at[3])
    store_key.start()
    store_ds.wait()
    store_value.wait()
    store_key.wait()


def outputs_kernel(
    place, stats, stats_up, stats_down, keys, features_far, keep_far, send_far, *rest
):
    parts, (features, low, gathered, sems) = rest[:4], rest[4:]
    quarter = parts[0].shape[0]
    half, rows = low.shape[1:]
    width = keys.shape[1]
    fetches = [
        pltpu.make_async_copy(far, near, sems.at[i])
        for i, (far, near) in enumerate(
            ((features_far, features), (keep_far, low.at[0]), (send_far, low.at[1]))
        )
    ]
    for f in fetches:
        f.start()
    peak, total, _ = merged((stats, stats_up, stats_down))
    share = jnp.exp(stats[0:1, :] - peak) / total
    share = jnp.transpose(jnp.broadcast_to(share, (128, rows)))
    share = jnp.concatenate([share] * (width // 128), axis=1)
    fetches[0].wait()
    gathered[:, width:] = (features[...].astype(F32) * share).astype(BF16)
    query = jnp.zeros((rows, width), F32)
    for i, at in enumerate((place[1], half - place[1])):
        fetches[i + 1].wait()
        right = keys[pl.ds(pl.multiple_of(at, half), half), :]
        query += lax.dot_general(low[i], right, TN, preferred_element_type=F32)
    gathered[:, :width] = (query * width ** (-0.5)).astype(BF16)
    for d, part in enumerate(parts):
        at = ((place[0] + d) & 3) * quarter
        part[...] = gathered[pl.ds(pl.multiple_of(at, quarter), quarter), :]


def add_kernel(keep_far, came_far, out, keep, came, sems):
    n = sems.shape[1]
    size = keep.shape[0] // n
    parts = [pl.ds(size * i, size) for i in range(n)]
    copy = pltpu.make_async_copy
    fetches = [
        (copy(keep_far.at[p], keep.at[p], sems.at[0, i]),
         copy(came_far.at[p], came.at[p], sems.at[1, i]))
        for i, p in enumerate(parts)
    ]
    stores = [copy(keep.at[p], out.at[p], sems.at[2, i]) for i, p in enumerate(parts)]
    for a, b in fetches:
        a.start()
        b.start()
    for i, p in enumerate(parts):
        for f in fetches[i]:
            f.wait()
        keep[p, :] = (keep[p, :].astype(F32) + came[p, :].astype(F32)).astype(BF16)
        stores[i].start()
    for store in stores:
        store.wait()


def sum_kernel(came, out):
    out[...] = f32_sum([came[j] for j in range(came.shape[0])]).astype(BF16)


def shifted(value, axis, d):
    n = lax.axis_size(axis)
    return lax.ppermute(value, axis, [(i, (i + d) % n) for i in range(n)])


def f32_sum(parts):
    total = parts[0].astype(F32)
    for part in parts[1:]:
        total = total + part.astype(F32)
    return total


def step(queries, keys, values, band_first, cotangent):
    rows, width = queries.shape
    own = keys.shape[0]
    phon = lax.axis_index("phon")
    core = lax.axis_index("frames") & 1
    n = lax.axis_size("frames")
    block = own * n
    half = block // 2
    ranks = lax.axis_size("phon")
    quarter = rows // ranks
    dma = pltpu.SemaphoreType.DMA
    near = [pltpu.VMEM((rows, width), BF16)] * 2

    both = jnp.concatenate([keys, values], axis=1).astype(F32) * LIFT
    every = lax.all_gather(both.astype(jnp.float16), "frames", axis=0, tiled=True)
    every = (every.astype(F32) * (1.0 / LIFT)).astype(BF16)
    tiles = phon * (block // TILE) + jnp.asarray(np.asarray(BLOCKS, np.int32) * own // TILE)
    flags = ((tiles >= band_first[0]) & (tiles < band_first[0] + NBAND)).astype(jnp.int32)
    work = 2 * block * rows * width
    block_keys, block_values, features, stats = call(
        forward_kernel,
        [((block, width), BF16, VMEM)] * 2 + [((rows, width), BF16, HBM), ((3, rows), F32, VMEM)],
        [(flags, SMEM), (every, VMEM), (queries, HBM), (cotangent, HBM)],
        [
            pltpu.VMEM((block, rows), F32),
            pltpu.VMEM((block, rows), BF16),
            *near,
            pltpu.VMEM((rows, width), BF16),
            dma((3,)),
        ],
        2 * work,
    )
    heard = [(stats, VMEM), (shifted(stats, "phon", 1), VMEM), (shifted(stats, "phon", 3), VMEM)]

    def backward(start):
        return call(
            backward_kernel,
            [((half, 2 * width), BF16, HBM), ((half, rows), BF16, HBM)],
            [
                (jnp.reshape(start, (1,)).astype(jnp.int32), SMEM),
                (flags, SMEM),
                *heard,
                (block_keys, VMEM),
                (block_values, VMEM),
                (queries, HBM),
                (cotangent, HBM),
            ],
            near
            + [
                pltpu.VMEM((half, 2 * width), BF16),
                pltpu.VMEM((half, rows), BF16),
                dma((5,)),
            ],
            2 * work,
        )

    send, send_ds = backward((1 - core) * half)
    came = lax.ppermute(send, "frames", [(i, i ^ 1) for i in range(n)])
    keep, keep_ds = backward(core * half)
    (first,) = call(
        add_kernel,
        [((half, 2 * width), BF16, HBM)],
        [(keep, HBM), (came, HBM)],
        [pltpu.VMEM((half, 2 * width), BF16)] * 2 + [dma((3, 4))],
    )
    first = lax.all_to_all(
        first.reshape(4, half // 4, 2 * width), "frames", 0, 0, tiled=True,
        axis_index_groups=QUADS,
    )

    place = jnp.stack([phon, core * half]).astype(jnp.int32)
    parts = call(
        outputs_kernel,
        [((quarter, 2 * width), BF16, VMEM)] * 4,
        [
            (place, SMEM),
            *heard,
            (block_keys, VMEM),
            (features, HBM),
            (keep_ds, HBM),
            (send_ds, HBM),
        ],
        [
            pltpu.VMEM((rows, width), BF16),
            pltpu.VMEM((2, half, rows), BF16),
            pltpu.VMEM((rows, 2 * width), BF16),
            dma((3,)),
        ],
        work,
    )
    moved = [parts[0]] + [shifted(parts[d], "phon", d) for d in (2, 1, 3)]

    (second,) = call(sum_kernel, [((half // 4, 2 * width), BF16, VMEM)], [(first, VMEM)])
    second = lax.all_to_all(
        second.reshape(4, own, 2 * width), "frames", 0, 0, tiled=True,
        axis_index_groups=CROSSES,
    )
    mine = f32_sum(moved).astype(BF16)
    spread = [mine] + [shifted(mine, "phon", d) for d in (1, 2, 3)]

    def placed(parts):
        whole = jnp.zeros((ranks, quarter, width), BF16)
        for d, p in enumerate(parts):
            whole = lax.dynamic_update_index_in_dim(whole, p, (phon - d) & 3, 0)
        return whole.reshape(rows, width)

    grad_query = placed([m[:, :width] for m in spread])
    aligned = placed([m[:, width:] for m in spread])
    grad = f32_sum([second[i] for i in range(4)])
    return (aligned, grad_query, grad[:, :width], grad[:, width:])


def solution(mesh):
    in_specs = (
        P(("chap", "frames"), None),
        P(("chap", "phon", "frames"), None),
        P(("chap", "phon", "frames"), None),
        P(("chap", "frames")),
        P(("chap", "frames"), None),
    )
    out_specs = (
        P(("chap", "frames"), None),
        P(("chap", "frames"), None),
        P(("chap", "phon", "frames"), None),
        P(("chap", "phon", "frames"), None),
    )
    return jax.shard_map(step, mesh=mesh, in_specs=in_specs, out_specs=out_specs, check_vma=False)
```

```python
import jax
import jax.numpy as jnp
import numpy as np
from jax import lax
from jax.experimental import pallas as pl
from jax.experimental.pallas import tpu as pltpu
from jax.sharding import PartitionSpec as P


TILE = 512
NBAND = 2
NEG_FILL = -1e30
FLOOR = -1e29
LIFT = 4096.0
CHUNK = 512
NT = (((1,), (1,)), ((), ()))
TN = (((0,), (0,)), ((), ()))
F32, BF16 = jnp.float32, jnp.bfloat16


def chip_order(offset):
    return [[(4 * g + (k + g) % 4 + offset) % 16 for g in range(4)] for k in range(4)]


ORDERS = [chip_order(0), chip_order(2)]
BLOCKS = [2 * ORDERS[c][k][g] + c for c in range(2) for k in range(4) for g in range(4)]
QUAD_STEPS = (2, 3, 1)
CROSS_STEPS = (2, 1, 3)
SPOTS = [(c, k, g) for c in range(2) for k in range(4) for g in range(4)]
MEMBER = {2 * ORDERS[c][k][g] + c: (k, g) for c, k, g in SPOTS}


def quad_mate(k, g, d):
    return (((k + g) % 4) ^ d) - g & 3


def quad_pairs(d):
    return [(2 * ORDERS[c][k][g] + c, 2 * ORDERS[c][quad_mate(k, g, d)][g] + c) for c, k, g in SPOTS]


def cross_pairs(d):
    return [(2 * ORDERS[c][k][g] + c, 2 * ORDERS[c][k][(g + d) % 4] + c) for c, k, g in SPOTS]


QUAD_ROWS = [[quad_mate(*MEMBER[f], d) for d in (0,) + QUAD_STEPS] for f in range(32)]
CROSS_ROWS = [[(MEMBER[f][1] + d) % 4 for d in (0,) + CROSS_STEPS] for f in range(32)]


VMEM, HBM, SMEM = pltpu.VMEM, pltpu.HBM, pltpu.SMEM


def call(kernel, outs, args, scratch=(), flops=0):
    shapes = [
        HBM(shape, dtype) if space == HBM else jax.ShapeDtypeStruct(shape, dtype)
        for shape, dtype, space in outs
    ]
    size = sum(a.size * a.dtype.itemsize for a, _ in args)
    size += sum(int(np.prod(o.shape)) * o.dtype.itemsize for o in shapes)
    return pl.pallas_call(
        kernel,
        out_shape=shapes,
        in_specs=[pl.BlockSpec(memory_space=space) for _, space in args],
        out_specs=[pl.BlockSpec(memory_space=space) for _, _, space in outs],
        scratch_shapes=list(scratch),
        cost_estimate=pl.CostEstimate(flops=flops, bytes_accessed=size, transcendentals=0),
        compiler_params=pltpu.CompilerParams(vmem_limit_bytes=16 << 20),
    )(*[pltpu.with_memory_space_constraint(a, HBM) if space == HBM else a for a, space in args])


def masked(scores, flags, first, own):
    return jnp.concatenate(
        [
            jnp.where(flags[first + j] > 0, scores[own * j : own * (j + 1)], NEG_FILL)
            for j in range(scores.shape[0] // own)
        ],
        axis=0,
    )


def forward_kernel(
    flags, every, queries_far, cotangent_far, keys, values, features_far, stats,
    scores_at, expd, queries, cotangent, features, sems,
):
    block, width = keys.shape
    own = block // len(BLOCKS)
    scale = width ** (-0.5)
    rows = queries.shape[0]
    fetch_q = pltpu.make_async_copy(queries_far, queries, sems.at[0])
    fetch_g = pltpu.make_async_copy(cotangent_far, cotangent, sems.at[1])
    fetch_q.start()
    fetch_g.start()
    peak = jnp.full((1, rows), FLOOR, F32)
    for at in range(0, block, CHUNK):
        for i in range(at // own, (at + CHUNK) // own):
            piece = every[own * BLOCKS[i] : own * (BLOCKS[i] + 1), :]
            keys[own * i : own * (i + 1), :] = piece[:, :width]
            values[own * i : own * (i + 1), :] = piece[:, width:]
        if at == 0:
            fetch_q.wait()
        here = slice(at, at + CHUNK)
        key = keys[here, :].astype(F32)
        offset = jnp.sum(key * key, axis=1, keepdims=True) * (-0.5 * scale)
        raw = lax.dot_general(keys[here, :], queries[...], NT, preferred_element_type=F32)
        scores = masked(raw * scale + offset, flags, at // own, own)
        scores_at[here, :] = scores
        peak = jnp.maximum(peak, jnp.max(scores, axis=0, keepdims=True))
    total = jnp.zeros_like(peak)
    for at in range(0, block, CHUNK):
        here = slice(at, at + CHUNK)
        e = jnp.exp(scores_at[here, :] - peak)
        expd[here, :] = e.astype(BF16)
        total += jnp.sum(e, axis=0, keepdims=True)
    out = lax.dot_general(expd[...], values[...], TN, preferred_element_type=F32)
    features[...] = out.astype(BF16)
    store_f = pltpu.make_async_copy(features, features_far, sems.at[2])
    store_f.start()
    fetch_g.wait()
    delta = jnp.sum(cotangent[...].astype(F32) * out, axis=1, keepdims=True)
    delta = jnp.transpose(jnp.broadcast_to(delta, (rows, 128)))[0:1, :]
    stats[0:1, :] = peak
    stats[1:2, :] = total
    stats[2:3, :] = delta
    store_f.wait()


def merged(heard):
    peaks = [stats[0:1, :] for stats in heard]
    peak = peaks[0]
    for p in peaks[1:]:
        peak = jnp.maximum(peak, p)
    weights = [jnp.exp(p - peak) for p in peaks]
    total = sum(w * stats[1:2, :] for w, stats in zip(weights, heard))
    delta = sum(w * stats[2:3, :] for w, stats in zip(weights, heard))
    return peak, jnp.maximum(total, 0.5), delta


def backward_kernel(
    start, flags, stats, stats_up, stats_down, keys, values, queries_far, cotangent_far,
    grads_out, ds_far, queries, cotangent, ds_low, sems, *room,
):
    grads = room[0] if room else grads_out
    half, width = grads.shape[0], keys.shape[1]
    scale = width ** (-0.5)
    own = 2 * half // len(BLOCKS)
    mine = pl.ds(pl.multiple_of(start[0], half), half)
    fetch_q = pltpu.make_async_copy(queries_far, queries, sems.at[0])
    fetch_g = pltpu.make_async_copy(cotangent_far, cotangent, sems.at[1])
    fetch_q.start()
    fetch_g.start()
    peak, total, delta = merged((stats, stats_up, stats_down))
    delta = delta / total
    lse = peak + jnp.log(total)
    low_key = keys[mine, :]
    key = low_key.astype(F32)
    offset = jnp.sum(key * key, axis=1, keepdims=True) * (-0.5 * scale)
    fetch_q.wait()
    raw = lax.dot_general(low_key, queries[...], NT, preferred_element_type=F32)
    fetch_g.wait()
    dp = lax.dot_general(values[mine, :], cotangent[...], NT, preferred_element_type=F32)
    scores = masked(raw * scale + offset, flags, start[0] // own, own)
    probs = jnp.exp(scores - lse)
    value = jnp.dot(probs.astype(BF16), cotangent[...], preferred_element_type=F32)
    grads[:, width:] = value.astype(BF16)
    right = pl.ds(width, width)
    stores = []
    if room:
        stores += [pltpu.make_async_copy(grads.at[:, right], grads_out.at[:, right], sems.at[4])]
        stores[-1].start()
    ds = probs * (dp - delta)
    low = ds.astype(BF16)
    ds_low[...] = low
    stores += [pltpu.make_async_copy(ds_low, ds_far, sems.at[2])]
    stores[-1].start()
    column = jnp.sum(ds, axis=1, keepdims=True)
    grad = jnp.dot(low, queries[...], preferred_element_type=F32)
    grads[:, :width] = ((grad - column * keys[mine, :].astype(F32)) * scale).astype(BF16)
    left = pl.ds(0, width)
    if room:
        stores += [pltpu.make_async_copy(grads.at[:, left], grads_out.at[:, left], sems.at[3])]
        stores[-1].start()
    for store in stores:
        store.wait()


def outputs_kernel(
    keep_at, stats, stats_up, stats_down, keys, features_far, keep_far, send_far, out,
    features, low, sems,
):
    half, rows = low.shape[1:]
    width = keys.shape[1]
    fetches = [
        pltpu.make_async_copy(far, near, sems.at[i])
        for i, (far, near) in enumerate(
            ((features_far, features), (keep_far, low.at[0]), (send_far, low.at[1]))
        )
    ]
    for f in fetches:
        f.start()
    peak, total, _ = merged((stats, stats_up, stats_down))
    share = jnp.exp(stats[0:1, :] - peak) / total
    share = jnp.transpose(jnp.broadcast_to(share, (128, rows)))
    share = jnp.concatenate([share] * (width // 128), axis=1)
    fetches[0].wait()
    out[:, width:] = (features[...].astype(F32) * share).astype(BF16)
    query = jnp.zeros((rows, width), F32)
    for i, at in enumerate((keep_at[0], half - keep_at[0])):
        fetches[i + 1].wait()
        right = keys[pl.ds(pl.multiple_of(at, half), half), :]
        query += lax.dot_general(low[i], right, TN, preferred_element_type=F32)
    out[:, :width] = (query * width ** (-0.5)).astype(BF16)


def add_kernel(order, keep, came, *outs):
    size = outs[0].shape[0]
    for i, out in enumerate(outs):
        part = pl.ds(pl.multiple_of(order[i] * size, size), size)
        out[...] = (keep[part, :].astype(F32) + came[part, :].astype(F32)).astype(BF16)


def sum_kernel(order, own, one, two, three, *outs):
    size = outs[0].shape[0]
    for i, out in enumerate(outs):
        part = pl.ds(pl.multiple_of(order[i] * size, size), size)
        out[...] = f32_sum([own[part, :], one[part, :], two[part, :], three[part, :]]).astype(BF16)


def mine_kernel(came, out):
    total = f32_sum([came[i] for i in range(came.shape[0])]).astype(BF16)
    for i in range(out.shape[0]):
        out[i] = total


def shifted(value, axis, d):
    n = lax.axis_size(axis)
    return lax.ppermute(value, axis, [(i, (i + d) % n) for i in range(n)])


def f32_sum(parts):
    total = parts[0].astype(F32)
    for part in parts[1:]:
        total = total + part.astype(F32)
    return total


def step(queries, keys, values, band_first, cotangent):
    rows, width = queries.shape
    own = keys.shape[0]
    phon = lax.axis_index("phon")
    core = lax.axis_index("frames") & 1
    n = lax.axis_size("frames")
    block = own * n
    half = block // 2
    ranks = lax.axis_size("phon")
    quarter = rows // ranks
    dma = pltpu.SemaphoreType.DMA
    near = [pltpu.VMEM((rows, width), BF16)] * 2

    both = jnp.concatenate([keys, values], axis=1).astype(F32) * LIFT
    every = lax.all_gather(both.astype(jnp.float16), "frames", axis=0, tiled=True)
    every = (every.astype(F32) * (1.0 / LIFT)).astype(BF16)
    tiles = phon * (block // TILE) + jnp.asarray(np.asarray(BLOCKS, np.int32) * own // TILE)
    flags = ((tiles >= band_first[0]) & (tiles < band_first[0] + NBAND)).astype(jnp.int32)
    work = 2 * block * rows * width
    block_keys, block_values, features, stats = call(
        forward_kernel,
        [((block, width), BF16, VMEM)] * 2 + [((rows, width), BF16, HBM), ((3, rows), F32, VMEM)],
        [(flags, SMEM), (every, VMEM), (queries, HBM), (cotangent, HBM)],
        [
            pltpu.VMEM((block, rows), F32),
            pltpu.VMEM((block, rows), BF16),
            *near,
            pltpu.VMEM((rows, width), BF16),
            dma((3,)),
        ],
        2 * work,
    )
    heard = [(stats, VMEM), (shifted(stats, "phon", 1), VMEM), (shifted(stats, "phon", 3), VMEM)]

    def backward(start, space=HBM):
        return call(
            backward_kernel,
            [((half, 2 * width), BF16, space), ((half, rows), BF16, HBM)],
            [
                (jnp.reshape(start, (1,)).astype(jnp.int32), SMEM),
                (flags, SMEM),
                *heard,
                (block_keys, VMEM),
                (block_values, VMEM),
                (queries, HBM),
                (cotangent, HBM),
            ],
            near
            + [pltpu.VMEM((half, rows), BF16), dma((5,))]
            + [pltpu.VMEM((half, 2 * width), BF16)] * (space == HBM),
            2 * work,
        )

    send, send_ds = backward((1 - core) * half)
    came = lax.ppermute(send, "frames", [(i, i ^ 1) for i in range(n)])
    keep, keep_ds = backward(core * half, VMEM)
    frame = lax.axis_index("frames")
    pick = lambda table: lax.dynamic_index_in_dim(jnp.asarray(table, jnp.int32), frame, 0, False)
    part = half // 4
    own_part, *parts = call(
        add_kernel,
        [((part, 2 * width), BF16, VMEM)] * 4,
        [(pick(QUAD_ROWS), SMEM), (keep, VMEM), (came, VMEM)],
    )
    parts = [lax.ppermute(p, "frames", quad_pairs(d)) for p, d in zip(parts, QUAD_STEPS)]

    (outs,) = call(
        outputs_kernel,
        [((rows, 2 * width), BF16, VMEM)],
        [
            (jnp.reshape(core * half, (1,)).astype(jnp.int32), SMEM),
            *heard,
            (block_keys, VMEM),
            (features, HBM),
            (keep_ds, HBM),
            (send_ds, HBM),
        ],
        [pltpu.VMEM((rows, width), BF16), pltpu.VMEM((2, half, rows), BF16), dma((3,))],
        work,
    )
    outs = lax.all_to_all(
        outs.reshape(ranks, quarter, 2 * width), "phon", 0, 0, tiled=True
    )

    own_grad, *grads = call(
        sum_kernel,
        [((own, 2 * width), BF16, VMEM)] * 4,
        [(pick(CROSS_ROWS), SMEM), (own_part, VMEM)] + [(p, VMEM) for p in parts],
    )
    grads = [lax.ppermute(g, "frames", cross_pairs(d)) for g, d in zip(grads, CROSS_STEPS)]
    (mine,) = call(mine_kernel, [((ranks, quarter, 2 * width), BF16, VMEM)], [(outs, VMEM)])
    outs = lax.all_to_all(mine, "phon", 0, 0, tiled=True).reshape(rows, 2 * width)
    grad = f32_sum([own_grad] + grads)
    return (outs[:, width:], outs[:, :width], grad[:, :width], grad[:, width:])


def solution(mesh):
    in_specs = (
        P(("chap", "frames"), None),
        P(("chap", "phon", "frames"), None),
        P(("chap", "phon", "frames"), None),
        P(("chap", "frames")),
        P(("chap", "frames"), None),
    )
    out_specs = (
        P(("chap", "frames"), None),
        P(("chap", "frames"), None),
        P(("chap", "phon", "frames"), None),
        P(("chap", "phon", "frames"), None),
    )
    return jax.shard_map(step, mesh=mesh, in_specs=in_specs, out_specs=out_specs, check_vma=False)
```

```python
import jax
import jax.numpy as jnp
import numpy as np
from jax import lax
from jax.experimental import pallas as pl
from jax.experimental.pallas import tpu as pltpu
from jax.sharding import PartitionSpec as P


TILE = 512
NBAND = 2
NEG_FILL = -1e30
FLOOR = -1e29
LIFT = 4096.0
CHUNK = 512
NT = (((1,), (1,)), ((), ()))
TN = (((0,), (0,)), ((), ()))
F32, BF16 = jnp.float32, jnp.bfloat16


def chip_order(offset):
    return [[(4 * g + (k + g) % 4 + offset) % 16 for g in range(4)] for k in range(4)]


ORDERS = [chip_order(0), chip_order(2)]
QUADS = [[2 * ORDERS[c][k][g] + c for k in range(4)] for c in range(2) for g in range(4)]
CROSSES = [[2 * ORDERS[c][k][g] + c for g in range(4)] for c in range(2) for k in range(4)]
BLOCKS = [2 * ORDERS[c][k][g] + c for c in range(2) for k in range(4) for g in range(4)]


VMEM, HBM, SMEM = pltpu.VMEM, pltpu.HBM, pltpu.SMEM


def call(kernel, outs, args, scratch=(), flops=0):
    shapes = [
        HBM(shape, dtype) if space == HBM else jax.ShapeDtypeStruct(shape, dtype)
        for shape, dtype, space in outs
    ]
    size = sum(a.size * a.dtype.itemsize for a, _ in args)
    size += sum(int(np.prod(o.shape)) * o.dtype.itemsize for o in shapes)
    return pl.pallas_call(
        kernel,
        out_shape=shapes,
        in_specs=[pl.BlockSpec(memory_space=space) for _, space in args],
        out_specs=[pl.BlockSpec(memory_space=space) for _, _, space in outs],
        scratch_shapes=list(scratch),
        cost_estimate=pl.CostEstimate(flops=flops, bytes_accessed=size, transcendentals=0),
        compiler_params=pltpu.CompilerParams(vmem_limit_bytes=16 << 20),
    )(*[pltpu.with_memory_space_constraint(a, HBM) if space == HBM else a for a, space in args])


def masked(scores, flags, first, own):
    return jnp.concatenate(
        [
            jnp.where(flags[first + j] > 0, scores[own * j : own * (j + 1)], NEG_FILL)
            for j in range(scores.shape[0] // own)
        ],
        axis=0,
    )


def forward_kernel(
    flags, every, queries_far, cotangent_far, keys, values, features_far, stats,
    scores_at, expd, queries, cotangent, features, sems,
):
    block, width = keys.shape
    own = block // len(BLOCKS)
    scale = width ** (-0.5)
    rows = queries.shape[0]
    fetch_q = pltpu.make_async_copy(queries_far, queries, sems.at[0])
    fetch_g = pltpu.make_async_copy(cotangent_far, cotangent, sems.at[1])
    fetch_q.start()
    fetch_g.start()
    peak = jnp.full((1, rows), FLOOR, F32)
    for at in range(0, block, CHUNK):
        for i in range(at // own, (at + CHUNK) // own):
            piece = every[own * BLOCKS[i] : own * (BLOCKS[i] + 1), :]
            keys[own * i : own * (i + 1), :] = piece[:, :width]
            values[own * i : own * (i + 1), :] = piece[:, width:]
        if at == 0:
            fetch_q.wait()
        here = slice(at, at + CHUNK)
        key = keys[here, :].astype(F32)
        offset = jnp.sum(key * key, axis=1, keepdims=True) * (-0.5 * scale)
        raw = lax.dot_general(keys[here, :], queries[...], NT, preferred_element_type=F32)
        scores = masked(raw * scale + offset, flags, at // own, own)
        scores_at[here, :] = scores
        peak = jnp.maximum(peak, jnp.max(scores, axis=0, keepdims=True))
    total = jnp.zeros_like(peak)
    for at in range(0, block, CHUNK):
        here = slice(at, at + CHUNK)
        e = jnp.exp(scores_at[here, :] - peak)
        expd[here, :] = e.astype(BF16)
        total += jnp.sum(e, axis=0, keepdims=True)
    out = lax.dot_general(expd[...], values[...], TN, preferred_element_type=F32)
    features[...] = out.astype(BF16)
    store_f = pltpu.make_async_copy(features, features_far, sems.at[2])
    store_f.start()
    fetch_g.wait()
    delta = jnp.sum(cotangent[...].astype(F32) * out, axis=1, keepdims=True)
    delta = jnp.transpose(jnp.broadcast_to(delta, (rows, 128)))[0:1, :]
    stats[0:1, :] = peak
    stats[1:2, :] = total
    stats[2:3, :] = delta
    store_f.wait()


def merged(heard):
    peaks = [stats[0:1, :] for stats in heard]
    peak = peaks[0]
    for p in peaks[1:]:
        peak = jnp.maximum(peak, p)
    weights = [jnp.exp(p - peak) for p in peaks]
    total = sum(w * stats[1:2, :] for w, stats in zip(weights, heard))
    delta = sum(w * stats[2:3, :] for w, stats in zip(weights, heard))
    return peak, jnp.maximum(total, 0.5), delta


def backward_kernel(
    start, flags, stats, stats_up, stats_down, keys, values, queries, cotangent_far,
    grads_out, ds_far, cotangent, ds_low, sems, *room,
):
    grads = room[0] if room else grads_out
    half, width = grads.shape[0], keys.shape[1]
    scale = width ** (-0.5)
    own = 2 * half // len(BLOCKS)
    mine = pl.ds(pl.multiple_of(start[0], half), half)
    fetch_g = pltpu.make_async_copy(cotangent_far, cotangent, sems.at[1])
    fetch_g.start()
    peak, total, delta = merged((stats, stats_up, stats_down))
    delta = delta / total
    lse = peak + jnp.log(total)
    low_key = keys[mine, :]
    key = low_key.astype(F32)
    offset = jnp.sum(key * key, axis=1, keepdims=True) * (-0.5 * scale)
    raw = lax.dot_general(low_key, queries[...], NT, preferred_element_type=F32)
    fetch_g.wait()
    dp = lax.dot_general(values[mine, :], cotangent[...], NT, preferred_element_type=F32)
    scores = masked(raw * scale + offset, flags, start[0] // own, own)
    probs = jnp.exp(scores - lse)
    value = jnp.dot(probs.astype(BF16), cotangent[...], preferred_element_type=F32)
    grads[:, width:] = value.astype(BF16)
    right = pl.ds(width, width)
    stores = []
    if room:
        stores += [pltpu.make_async_copy(grads.at[:, right], grads_out.at[:, right], sems.at[4])]
        stores[-1].start()
    ds = probs * (dp - delta)
    low = ds.astype(BF16)
    ds_low[...] = low
    stores += [pltpu.make_async_copy(ds_low, ds_far, sems.at[2])]
    stores[-1].start()
    column = jnp.sum(ds, axis=1, keepdims=True)
    grad = jnp.dot(low, queries[...], preferred_element_type=F32)
    grads[:, :width] = ((grad - column * keys[mine, :].astype(F32)) * scale).astype(BF16)
    left = pl.ds(0, width)
    if room:
        stores += [pltpu.make_async_copy(grads.at[:, left], grads_out.at[:, left], sems.at[3])]
        stores[-1].start()
    for store in stores:
        store.wait()


def outputs_kernel(
    place, stats, stats_up, stats_down, keys, features_far, keep_far, send_far, *rest
):
    parts, (features, low, gathered, sems) = rest[:4], rest[4:]
    quarter = parts[0].shape[0]
    half, rows = low.shape[1:]
    width = keys.shape[1]
    fetches = [
        pltpu.make_async_copy(far, near, sems.at[i])
        for i, (far, near) in enumerate(
            ((features_far, features), (keep_far, low.at[0]), (send_far, low.at[1]))
        )
    ]
    for f in fetches:
        f.start()
    peak, total, _ = merged((stats, stats_up, stats_down))
    share = jnp.exp(stats[0:1, :] - peak) / total
    share = jnp.transpose(jnp.broadcast_to(share, (128, rows)))
    share = jnp.concatenate([share] * (width // 128), axis=1)
    fetches[0].wait()
    gathered[:, width:] = (features[...].astype(F32) * share).astype(BF16)
    query = jnp.zeros((rows, width), F32)
    for i, at in enumerate((place[1], half - place[1])):
        fetches[i + 1].wait()
        right = keys[pl.ds(pl.multiple_of(at, half), half), :]
        query += lax.dot_general(low[i], right, TN, preferred_element_type=F32)
    gathered[:, :width] = (query * width ** (-0.5)).astype(BF16)
    for d, part in enumerate(parts):
        at = ((place[0] + d) & 3) * quarter
        part[...] = gathered[pl.ds(pl.multiple_of(at, quarter), quarter), :]


def add_kernel(keep, came_far, out, came, sems):
    n = sems.shape[1]
    size = keep.shape[0] // n
    parts = [pl.ds(size * i, size) for i in range(n)]
    copy = pltpu.make_async_copy
    fetches = [copy(came_far.at[p], came.at[p], sems.at[0, i]) for i, p in enumerate(parts)]
    stores = [copy(came.at[p], out.at[p], sems.at[1, i]) for i, p in enumerate(parts)]
    for fetch in fetches:
        fetch.start()
    for i, p in enumerate(parts):
        fetches[i].wait()
        came[p, :] = (keep[p, :].astype(F32) + came[p, :].astype(F32)).astype(BF16)
        stores[i].start()
    for store in stores:
        store.wait()


def sum_kernel(came, out):
    out[...] = f32_sum([came[j] for j in range(came.shape[0])]).astype(BF16)


def shifted(value, axis, d):
    n = lax.axis_size(axis)
    return lax.ppermute(value, axis, [(i, (i + d) % n) for i in range(n)])


def f32_sum(parts):
    total = parts[0].astype(F32)
    for part in parts[1:]:
        total = total + part.astype(F32)
    return total


def step(queries, keys, values, band_first, cotangent):
    rows, width = queries.shape
    own = keys.shape[0]
    phon = lax.axis_index("phon")
    core = lax.axis_index("frames") & 1
    n = lax.axis_size("frames")
    block = own * n
    half = block // 2
    ranks = lax.axis_size("phon")
    quarter = rows // ranks
    dma = pltpu.SemaphoreType.DMA
    near = [pltpu.VMEM((rows, width), BF16)] * 2

    both = jnp.concatenate([keys, values], axis=1).astype(F32) * LIFT
    every = lax.all_gather(both.astype(jnp.float16), "frames", axis=0, tiled=True)
    every = (every.astype(F32) * (1.0 / LIFT)).astype(BF16)
    tiles = phon * (block // TILE) + jnp.asarray(np.asarray(BLOCKS, np.int32) * own // TILE)
    flags = ((tiles >= band_first[0]) & (tiles < band_first[0] + NBAND)).astype(jnp.int32)
    work = 2 * block * rows * width
    block_keys, block_values, features, stats = call(
        forward_kernel,
        [((block, width), BF16, VMEM)] * 2 + [((rows, width), BF16, HBM), ((3, rows), F32, VMEM)],
        [(flags, SMEM), (every, VMEM), (queries, HBM), (cotangent, HBM)],
        [
            pltpu.VMEM((block, rows), F32),
            pltpu.VMEM((block, rows), BF16),
            *near,
            pltpu.VMEM((rows, width), BF16),
            dma((3,)),
        ],
        2 * work,
    )
    heard = [(stats, VMEM), (shifted(stats, "phon", 1), VMEM), (shifted(stats, "phon", 3), VMEM)]

    def backward(start, space=HBM):
        return call(
            backward_kernel,
            [((half, 2 * width), BF16, space), ((half, rows), BF16, HBM)],
            [
                (jnp.reshape(start, (1,)).astype(jnp.int32), SMEM),
                (flags, SMEM),
                *heard,
                (block_keys, VMEM),
                (block_values, VMEM),
                (queries, VMEM),
                (cotangent, HBM),
            ],
            near[1:]
            + [pltpu.VMEM((half, rows), BF16), dma((5,))]
            + [pltpu.VMEM((half, 2 * width), BF16)] * (space == HBM),
            2 * work,
        )

    send, send_ds = backward((1 - core) * half)
    came = lax.ppermute(send, "frames", [(i, i ^ 1) for i in range(n)])
    keep, keep_ds = backward(core * half, VMEM)
    (first,) = call(
        add_kernel,
        [((half, 2 * width), BF16, HBM)],
        [(keep, VMEM), (came, HBM)],
        [pltpu.VMEM((half, 2 * width), BF16), dma((2, 4))],
    )
    first = lax.all_to_all(
        first.reshape(4, half // 4, 2 * width), "frames", 0, 0, tiled=True,
        axis_index_groups=QUADS,
    )

    place = jnp.stack([phon, core * half]).astype(jnp.int32)
    parts = call(
        outputs_kernel,
        [((quarter, 2 * width), BF16, VMEM)] * 4,
        [
            (place, SMEM),
            *heard,
            (block_keys, VMEM),
            (features, HBM),
            (keep_ds, HBM),
            (send_ds, HBM),
        ],
        [
            pltpu.VMEM((rows, width), BF16),
            pltpu.VMEM((2, half, rows), BF16),
            pltpu.VMEM((rows, 2 * width), BF16),
            dma((3,)),
        ],
        work,
    )
    moved = [parts[0]] + [shifted(parts[d], "phon", d) for d in (2, 1, 3)]

    (second,) = call(sum_kernel, [((half // 4, 2 * width), BF16, VMEM)], [(first, VMEM)])
    second = lax.all_to_all(
        second.reshape(4, own, 2 * width), "frames", 0, 0, tiled=True,
        axis_index_groups=CROSSES,
    )
    mine = f32_sum(moved).astype(BF16)
    spread = [mine] + [shifted(mine, "phon", d) for d in (2, 3, 1)]

    def placed(parts):
        whole = jnp.zeros((ranks, quarter, width), BF16)
        for d, p in zip((0, 2, 3, 1), parts):
            whole = lax.dynamic_update_index_in_dim(whole, p, (phon - d) & 3, 0)
        return whole.reshape(rows, width)

    grad_query = placed([m[:, :width] for m in spread])
    aligned = placed([m[:, width:] for m in spread])
    grad = f32_sum([second[i] for i in range(4)])
    return (aligned, grad_query, grad[:, :width], grad[:, width:])


def solution(mesh):
    in_specs = (
        P(("chap", "frames"), None),
        P(("chap", "phon", "frames"), None),
        P(("chap", "phon", "frames"), None),
        P(("chap", "frames")),
        P(("chap", "frames"), None),
    )
    out_specs = (
        P(("chap", "frames"), None),
        P(("chap", "frames"), None),
        P(("chap", "phon", "frames"), None),
        P(("chap", "phon", "frames"), None),
    )
    return jax.shard_map(step, mesh=mesh, in_specs=in_specs, out_specs=out_specs, check_vma=False)
```

```python
import jax
import jax.numpy as jnp
import numpy as np
from jax import lax
from jax.experimental import pallas as pl
from jax.experimental.pallas import tpu as pltpu
from jax.sharding import PartitionSpec as P


TILE = 512
NBAND = 2
NEG_FILL = -1e30
FLOOR = -1e29
LIFT = 4096.0
NT = (((1,), (1,)), ((), ()))
TN = (((0,), (0,)), ((), ()))
F32, BF16 = jnp.float32, jnp.bfloat16


def chip_order(offset):
    return [[(4 * g + (k + g) % 4 + offset) % 16 for g in range(4)] for k in range(4)]


ORDERS = [chip_order(0), chip_order(2)]
QUADS = [[2 * ORDERS[c][k][g] + c for k in range(4)] for c in range(2) for g in range(4)]
CROSSES = [[2 * ORDERS[c][k][g] + c for g in range(4)] for c in range(2) for k in range(4)]
BLOCKS = [2 * ORDERS[c][k][g] + c for c in range(2) for k in range(4) for g in range(4)]


VMEM, HBM, SMEM = pltpu.VMEM, pltpu.HBM, pltpu.SMEM


def call(kernel, outs, args, scratch=(), flops=0):
    shapes = [
        HBM(shape, dtype) if space == HBM else jax.ShapeDtypeStruct(shape, dtype)
        for shape, dtype, space in outs
    ]
    size = sum(a.size * a.dtype.itemsize for a, _ in args)
    size += sum(int(np.prod(o.shape)) * o.dtype.itemsize for o in shapes)
    return pl.pallas_call(
        kernel,
        out_shape=shapes,
        in_specs=[pl.BlockSpec(memory_space=space) for _, space in args],
        out_specs=[pl.BlockSpec(memory_space=space) for _, _, space in outs],
        scratch_shapes=list(scratch),
        cost_estimate=pl.CostEstimate(flops=flops, bytes_accessed=size, transcendentals=0),
        compiler_params=pltpu.CompilerParams(vmem_limit_bytes=16 << 20),
    )(*[pltpu.with_memory_space_constraint(a, HBM) if space == HBM else a for a, space in args])


def half_rows(every, core, own, columns):
    count = len(BLOCKS) // 2
    rows = []
    for i in range(count):
        at = ((BLOCKS[i] + 4 * core) & (2 * count - 1)) + core
        rows.append(every[pl.ds(pl.multiple_of(at * own, own), own), columns])
    return jnp.concatenate(rows, axis=0)


def masked_half(scores, flags, core, own):
    count = len(BLOCKS) // 2
    parts = []
    for i in range(count):
        at = ((BLOCKS[i] + 4 * core) & (2 * count - 1)) + core
        parts.append(
            jnp.where(flags[at * own // TILE] > 0, scores[own * i : own * (i + 1)], NEG_FILL)
        )
    return jnp.concatenate(parts, axis=0)


def forward_kernel(
    flags, every, queries, cotangent_far, features_far, stats,
    scores_at, expd, cotangent, features, sems,
):
    block = every.shape[0]
    rows, width = queries.shape
    scale = width ** (-0.5)
    fetch_g = pltpu.make_async_copy(cotangent_far, cotangent, sems.at[0])
    fetch_g.start()
    peak = jnp.full((1, rows), FLOOR, F32)
    for tile in range(block // TILE):
        here = slice(tile * TILE, (tile + 1) * TILE)
        low_key = every[here, :width]
        key = low_key.astype(F32)
        offset = jnp.sum(key * key, axis=1, keepdims=True) * (-0.5 * scale)
        raw = lax.dot_general(low_key, queries[...], NT, preferred_element_type=F32)
        scores = jnp.where(flags[tile] > 0, raw * scale + offset, NEG_FILL)
        scores_at[here, :] = scores
        peak = jnp.maximum(peak, jnp.max(scores, axis=0, keepdims=True))
    total = jnp.zeros_like(peak)
    for tile in range(block // TILE):
        here = slice(tile * TILE, (tile + 1) * TILE)
        e = jnp.exp(scores_at[here, :] - peak)
        expd[here, :] = e.astype(BF16)
        total += jnp.sum(e, axis=0, keepdims=True)
    deltas, stores = [], []
    for i in range(2):
        part = pl.ds(i * rows // 2, rows // 2)
        out = lax.dot_general(expd[:, part], every[:, width:], TN, preferred_element_type=F32)
        features[part, :] = out.astype(BF16)
        copy = pltpu.make_async_copy(features.at[part], features_far.at[part], sems.at[1 + i])
        copy.start()
        stores.append(copy)
        if i == 0:
            fetch_g.wait()
        delta = jnp.sum(cotangent[part, :].astype(F32) * out, axis=1, keepdims=True)
        deltas.append(jnp.transpose(jnp.broadcast_to(delta, (rows // 2, 128)))[0:1, :])
    delta = jnp.concatenate(deltas, axis=1)
    stats[0:1, :] = peak
    stats[1:2, :] = total
    stats[2:3, :] = delta
    for copy in stores:
        copy.wait()


def merged(heard):
    peaks = [stats[0:1, :] for stats in heard]
    peak = peaks[0]
    for p in peaks[1:]:
        peak = jnp.maximum(peak, p)
    weights = [jnp.exp(p - peak) for p in peaks]
    total = sum(w * stats[1:2, :] for w, stats in zip(weights, heard))
    delta = sum(w * stats[2:3, :] for w, stats in zip(weights, heard))
    return peak, jnp.maximum(total, 0.5), delta


def backward_kernel(
    side, flags, stats, stats_up, stats_down, every, queries, cotangent_far,
    grads_out, ds_far, cotangent, ds_low, sems, *room,
):
    grads = room[0] if room else grads_out
    width = queries.shape[1]
    scale = width ** (-0.5)
    own = every.shape[0] // len(BLOCKS)
    core = side[0]
    fetch_g = pltpu.make_async_copy(cotangent_far, cotangent, sems.at[1])
    fetch_g.start()
    peak, total, delta = merged((stats, stats_up, stats_down))
    delta = delta / total
    lse = peak + jnp.log(total)
    low_key = half_rows(every, core, own, slice(0, width))
    key = low_key.astype(F32)
    offset = jnp.sum(key * key, axis=1, keepdims=True) * (-0.5 * scale)
    raw = lax.dot_general(low_key, queries[...], NT, preferred_element_type=F32)
    fetch_g.wait()
    low_value = half_rows(every, core, own, slice(width, 2 * width))
    dp = lax.dot_general(low_value, cotangent[...], NT, preferred_element_type=F32)
    scores = masked_half(raw * scale + offset, flags, core, own)
    probs = jnp.exp(scores - lse)
    value = jnp.dot(probs.astype(BF16), cotangent[...], preferred_element_type=F32)
    grads[:, width:] = value.astype(BF16)
    right = pl.ds(width, width)
    stores = []
    if room:
        stores += [pltpu.make_async_copy(grads.at[:, right], grads_out.at[:, right], sems.at[4])]
        stores[-1].start()
    ds = probs * (dp - delta)
    low = ds.astype(BF16)
    ds_low[...] = low
    stores += [pltpu.make_async_copy(ds_low, ds_far, sems.at[2])]
    stores[-1].start()
    column = jnp.sum(ds, axis=1, keepdims=True)
    grad = jnp.dot(low, queries[...], preferred_element_type=F32)
    grads[:, :width] = ((grad - column * low_key.astype(F32)) * scale).astype(BF16)
    left = pl.ds(0, width)
    if room:
        stores += [pltpu.make_async_copy(grads.at[:, left], grads_out.at[:, left], sems.at[3])]
        stores[-1].start()
    for store in stores:
        store.wait()


def outputs_kernel(
    place, stats, stats_up, stats_down, every, features_far, keep_far, send_far, *rest
):
    parts, (features, low, gathered, sems) = rest[:4], rest[4:]
    quarter = parts[0].shape[0]
    rows, width = features.shape
    own = every.shape[0] // len(BLOCKS)
    fetches = [
        pltpu.make_async_copy(far, near, sems.at[i])
        for i, (far, near) in enumerate(
            ((features_far, features), (keep_far, low.at[0]), (send_far, low.at[1]))
        )
    ]
    for f in fetches:
        f.start()
    peak, total, _ = merged((stats, stats_up, stats_down))
    share = jnp.exp(stats[0:1, :] - peak) / total
    share = jnp.transpose(jnp.broadcast_to(share, (128, rows)))
    share = jnp.concatenate([share] * (width // 128), axis=1)
    fetches[0].wait()
    gathered[:, width:] = (features[...].astype(F32) * share).astype(BF16)
    query = jnp.zeros((rows, width), F32)
    for i, core in enumerate((place[1], 1 - place[1])):
        fetches[i + 1].wait()
        right = half_rows(every, core, own, slice(0, width))
        query += lax.dot_general(low[i], right, TN, preferred_element_type=F32)
    gathered[:, :width] = (query * width ** (-0.5)).astype(BF16)
    for d, part in enumerate(parts):
        at = ((place[0] + d) & 3) * quarter
        part[...] = gathered[pl.ds(pl.multiple_of(at, quarter), quarter), :]


def add_kernel(keep, came, out, made, sems):
    n = sems.shape[0]
    size = keep.shape[0] // n
    stores = []
    for i in range(n):
        part = pl.ds(size * i, size)
        made[part, :] = (keep[part, :].astype(F32) + came[part, :].astype(F32)).astype(BF16)
        stores.append(pltpu.make_async_copy(made.at[part], out.at[part], sems.at[i]))
        stores[-1].start()
    for store in stores:
        store.wait()


def sum_kernel(came, out):
    out[...] = f32_sum([came[j] for j in range(came.shape[0])]).astype(BF16)


def shifted(value, axis, d):
    n = lax.axis_size(axis)
    return lax.ppermute(value, axis, [(i, (i + d) % n) for i in range(n)])


def f32_sum(parts):
    total = parts[0].astype(F32)
    for part in parts[1:]:
        total = total + part.astype(F32)
    return total


def step(queries, keys, values, band_first, cotangent):
    rows, width = queries.shape
    own = keys.shape[0]
    phon = lax.axis_index("phon")
    core = lax.axis_index("frames") & 1
    n = lax.axis_size("frames")
    block = own * n
    half = block // 2
    ranks = lax.axis_size("phon")
    quarter = rows // ranks
    dma = pltpu.SemaphoreType.DMA
    near = [pltpu.VMEM((rows, width), BF16)] * 2

    both = jnp.concatenate([keys, values], axis=1).astype(F32) * LIFT
    every = lax.all_gather(both.astype(jnp.float16), "frames", axis=0, tiled=True)
    every = (every.astype(F32) * (1.0 / LIFT)).astype(BF16)
    tiles = phon * (block // TILE) + jnp.arange(block // TILE, dtype=jnp.int32)
    flags = ((tiles >= band_first[0]) & (tiles < band_first[0] + NBAND)).astype(jnp.int32)
    work = 2 * block * rows * width
    features, stats = call(
        forward_kernel,
        [((rows, width), BF16, HBM), ((3, rows), F32, VMEM)],
        [(flags, SMEM), (every, VMEM), (queries, VMEM), (cotangent, HBM)],
        [
            pltpu.VMEM((block, rows), F32),
            pltpu.VMEM((block, rows), BF16),
            near[0],
            pltpu.VMEM((rows, width), BF16),
            dma((3,)),
        ],
        2 * work,
    )
    heard = [(stats, VMEM), (shifted(stats, "phon", 1), VMEM), (shifted(stats, "phon", 3), VMEM)]

    def backward(side, space=HBM):
        return call(
            backward_kernel,
            [((half, 2 * width), BF16, space), ((half, rows), BF16, HBM)],
            [
                (jnp.reshape(side, (1,)).astype(jnp.int32), SMEM),
                (flags, SMEM),
                *heard,
                (every, VMEM),
                (queries, VMEM),
                (cotangent, HBM),
            ],
            near[1:]
            + [pltpu.VMEM((half, rows), BF16), dma((5,))]
            + [pltpu.VMEM((half, 2 * width), BF16)] * (space == HBM),
            2 * work,
        )

    send, send_ds = backward(1 - core)
    came = lax.ppermute(send, "frames", [(i, i ^ 1) for i in range(n)])
    keep, keep_ds = backward(core, VMEM)
    (first,) = call(
        add_kernel,
        [((half, 2 * width), BF16, HBM)],
        [(keep, VMEM), (came, VMEM)],
        [pltpu.VMEM((half, 2 * width), BF16), dma((4,))],
    )
    first = lax.all_to_all(
        first.reshape(4, half // 4, 2 * width), "frames", 0, 0, tiled=True,
        axis_index_groups=QUADS,
    )

    place = jnp.stack([phon, core]).astype(jnp.int32)
    parts = call(
        outputs_kernel,
        [((quarter, 2 * width), BF16, VMEM)] * 4,
        [
            (place, SMEM),
            *heard,
            (every, VMEM),
            (features, HBM),
            (keep_ds, HBM),
            (send_ds, HBM),
        ],
        [
            pltpu.VMEM((rows, width), BF16),
            pltpu.VMEM((2, half, rows), BF16),
            pltpu.VMEM((rows, 2 * width), BF16),
            dma((3,)),
        ],
        work,
    )
    moved = [parts[0]] + [shifted(parts[d], "phon", d) for d in (2, 1, 3)]

    (second,) = call(sum_kernel, [((half // 4, 2 * width), BF16, VMEM)], [(first, VMEM)])
    second = lax.all_to_all(
        second.reshape(4, own, 2 * width), "frames", 0, 0, tiled=True,
        axis_index_groups=CROSSES,
    )
    mine = f32_sum(moved).astype(BF16)
    spread = [mine] + [shifted(mine, "phon", d) for d in (2, 3, 1)]

    def placed(parts):
        whole = jnp.zeros((ranks, quarter, width), BF16)
        for d, p in zip((0, 2, 3, 1), parts):
            whole = lax.dynamic_update_index_in_dim(whole, p, (phon - d) & 3, 0)
        return whole.reshape(rows, width)

    grad_query = placed([m[:, :width] for m in spread])
    aligned = placed([m[:, width:] for m in spread])
    grad = f32_sum([second[i] for i in range(4)])
    return (aligned, grad_query, grad[:, :width], grad[:, width:])


def solution(mesh):
    in_specs = (
        P(("chap", "frames"), None),
        P(("chap", "phon", "frames"), None),
        P(("chap", "phon", "frames"), None),
        P(("chap", "frames")),
        P(("chap", "frames"), None),
    )
    out_specs = (
        P(("chap", "frames"), None),
        P(("chap", "frames"), None),
        P(("chap", "phon", "frames"), None),
        P(("chap", "phon", "frames"), None),
    )
    return jax.shard_map(step, mesh=mesh, in_specs=in_specs, out_specs=out_specs, check_vma=False)
```

```python
import jax
import jax.numpy as jnp
import numpy as np
from jax import lax
from jax.experimental import pallas as pl
from jax.experimental.pallas import tpu as pltpu
from jax.sharding import PartitionSpec as P


TILE = 512
NBAND = 2
NEG_FILL = -1e30
FLOOR = -1e29
LIFT = 4096.0
NT = (((1,), (1,)), ((), ()))
TN = (((0,), (0,)), ((), ()))
F32, BF16 = jnp.float32, jnp.bfloat16


def chip_order(offset):
    return [[(4 * g + (k + g) % 4 + offset) % 16 for g in range(4)] for k in range(4)]


ORDERS = [chip_order(0), chip_order(2)]
QUADS = [[2 * ORDERS[c][k][g] + c for k in range(4)] for c in range(2) for g in range(4)]
CROSSES = [[2 * ORDERS[c][k][g] + c for g in range(4)] for c in range(2) for k in range(4)]
BLOCKS = [2 * ORDERS[c][k][g] + c for c in range(2) for k in range(4) for g in range(4)]


VMEM, HBM, SMEM = pltpu.VMEM, pltpu.HBM, pltpu.SMEM


def call(kernel, outs, args, scratch=(), flops=0):
    shapes = [
        HBM(shape, dtype) if space == HBM else jax.ShapeDtypeStruct(shape, dtype)
        for shape, dtype, space in outs
    ]
    size = sum(a.size * a.dtype.itemsize for a, _ in args)
    size += sum(int(np.prod(o.shape)) * o.dtype.itemsize for o in shapes)
    return pl.pallas_call(
        kernel,
        out_shape=shapes,
        in_specs=[pl.BlockSpec(memory_space=space) for _, space in args],
        out_specs=[pl.BlockSpec(memory_space=space) for _, _, space in outs],
        scratch_shapes=list(scratch),
        cost_estimate=pl.CostEstimate(flops=flops, bytes_accessed=size, transcendentals=0),
        compiler_params=pltpu.CompilerParams(vmem_limit_bytes=16 << 20),
    )(*[pltpu.with_memory_space_constraint(a, HBM) if space == HBM else a for a, space in args])


def half_rows(every, core, own, columns):
    count = len(BLOCKS) // 2
    rows = []
    for i in range(count):
        at = ((BLOCKS[i] + 4 * core) & (2 * count - 1)) + core
        rows.append(every[pl.ds(pl.multiple_of(at * own, own), own), columns])
    return jnp.concatenate(rows, axis=0)


def masked_half(scores, flags, core, own):
    count = len(BLOCKS) // 2
    parts = []
    for i in range(count):
        at = ((BLOCKS[i] + 4 * core) & (2 * count - 1)) + core
        parts.append(
            jnp.where(flags[at * own // TILE] > 0, scores[own * i : own * (i + 1)], NEG_FILL)
        )
    return jnp.concatenate(parts, axis=0)


def forward_kernel(
    flags, every, queries, cotangent_far, features_far, stats,
    scores_at, expd, cotangent, features, sems,
):
    block = every.shape[0]
    rows, width = queries.shape
    scale = width ** (-0.5)
    fetch_g = pltpu.make_async_copy(cotangent_far, cotangent, sems.at[0])
    fetch_g.start()
    peak = jnp.full((1, rows), FLOOR, F32)
    for tile in range(block // TILE):
        here = slice(tile * TILE, (tile + 1) * TILE)
        low_key = every[here, :width]
        key = low_key.astype(F32)
        offset = jnp.sum(key * key, axis=1, keepdims=True) * (-0.5 * scale)
        raw = lax.dot_general(low_key, queries[...], NT, preferred_element_type=F32)
        scores = jnp.where(flags[tile] > 0, raw * scale + offset, NEG_FILL)
        scores_at[here, :] = scores
        peak = jnp.maximum(peak, jnp.max(scores, axis=0, keepdims=True))
    total = jnp.zeros_like(peak)
    for tile in range(block // TILE):
        here = slice(tile * TILE, (tile + 1) * TILE)
        e = jnp.exp(scores_at[here, :] - peak)
        expd[here, :] = e.astype(BF16)
        total += jnp.sum(e, axis=0, keepdims=True)
    deltas, stores = [], []
    for i in range(2):
        part = pl.ds(i * rows // 2, rows // 2)
        out = lax.dot_general(expd[:, part], every[:, width:], TN, preferred_element_type=F32)
        features[part, :] = out.astype(BF16)
        copy = pltpu.make_async_copy(features.at[part], features_far.at[part], sems.at[1 + i])
        copy.start()
        stores.append(copy)
        if i == 0:
            fetch_g.wait()
        delta = jnp.sum(cotangent[part, :].astype(F32) * out, axis=1, keepdims=True)
        deltas.append(jnp.transpose(jnp.broadcast_to(delta, (rows // 2, 128)))[0:1, :])
    delta = jnp.concatenate(deltas, axis=1)
    stats[0:1, :] = peak
    stats[1:2, :] = total
    stats[2:3, :] = delta
    for copy in stores:
        copy.wait()


def merged(heard):
    peaks = [stats[0:1, :] for stats in heard]
    peak = peaks[0]
    for p in peaks[1:]:
        peak = jnp.maximum(peak, p)
    weights = [jnp.exp(p - peak) for p in peaks]
    total = sum(w * stats[1:2, :] for w, stats in zip(weights, heard))
    delta = sum(w * stats[2:3, :] for w, stats in zip(weights, heard))
    return peak, jnp.maximum(total, 0.5), delta


def backward_kernel(
    side, flags, stats, stats_up, stats_down, every, queries, cotangent_far,
    grads_out, ds_far, cotangent, ds_low, sems, *room,
):
    grads = room[0] if room else grads_out
    width = queries.shape[1]
    scale = width ** (-0.5)
    own = every.shape[0] // len(BLOCKS)
    core = side[0]
    fetch_g = pltpu.make_async_copy(cotangent_far, cotangent, sems.at[1])
    fetch_g.start()
    peak, total, delta = merged((stats, stats_up, stats_down))
    delta = delta / total
    lse = peak + jnp.log(total)
    low_key = half_rows(every, core, own, slice(0, width))
    key = low_key.astype(F32)
    offset = jnp.sum(key * key, axis=1, keepdims=True) * (-0.5 * scale)
    raw = lax.dot_general(low_key, queries[...], NT, preferred_element_type=F32)
    fetch_g.wait()
    low_value = half_rows(every, core, own, slice(width, 2 * width))
    dp = lax.dot_general(low_value, cotangent[...], NT, preferred_element_type=F32)
    scores = masked_half(raw * scale + offset, flags, core, own)
    probs = jnp.exp(scores - lse)
    value = jnp.dot(probs.astype(BF16), cotangent[...], preferred_element_type=F32)
    grads[:, width:] = value.astype(BF16)
    right = pl.ds(width, width)
    stores = []
    if room:
        stores += [pltpu.make_async_copy(grads.at[:, right], grads_out.at[:, right], sems.at[4])]
        stores[-1].start()
    ds = probs * (dp - delta)
    low = ds.astype(BF16)
    ds_low[...] = low
    stores += [pltpu.make_async_copy(ds_low, ds_far, sems.at[2])]
    stores[-1].start()
    column = jnp.sum(ds, axis=1, keepdims=True)
    grad = jnp.dot(low, queries[...], preferred_element_type=F32)
    grads[:, :width] = ((grad - column * low_key.astype(F32)) * scale).astype(BF16)
    left = pl.ds(0, width)
    if room:
        stores += [pltpu.make_async_copy(grads.at[:, left], grads_out.at[:, left], sems.at[3])]
        stores[-1].start()
    for store in stores:
        store.wait()


def outputs_kernel(
    place, stats, stats_up, stats_down, every, features_far, keep_far, send_far, *rest
):
    parts, (features, low, gathered, sems) = rest[:4], rest[4:]
    quarter = parts[0].shape[0]
    rows, width = features.shape
    own = every.shape[0] // len(BLOCKS)
    fetches = [
        pltpu.make_async_copy(far, near, sems.at[i])
        for i, (far, near) in enumerate(
            ((features_far, features), (keep_far, low.at[0]), (send_far, low.at[1]))
        )
    ]
    for f in fetches:
        f.start()
    peak, total, _ = merged((stats, stats_up, stats_down))
    share = jnp.exp(stats[0:1, :] - peak) / total
    share = jnp.transpose(jnp.broadcast_to(share, (128, rows)))
    share = jnp.concatenate([share] * (width // 128), axis=1)
    fetches[0].wait()
    gathered[:, width:] = (features[...].astype(F32) * share).astype(BF16)
    query = jnp.zeros((rows, width), F32)
    for i, core in enumerate((place[1], 1 - place[1])):
        fetches[i + 1].wait()
        right = half_rows(every, core, own, slice(0, width))
        query += lax.dot_general(low[i], right, TN, preferred_element_type=F32)
    gathered[:, :width] = (query * width ** (-0.5)).astype(BF16)
    for d, part in enumerate(parts):
        at = (place[0] ^ d) * quarter
        part[...] = gathered[pl.ds(pl.multiple_of(at, quarter), quarter), :]


def add_kernel(keep, came, out, made, sems):
    n = sems.shape[0]
    size = keep.shape[0] // n
    stores = []
    for i in range(n):
        part = pl.ds(size * i, size)
        made[part, :] = (keep[part, :].astype(F32) + came[part, :].astype(F32)).astype(BF16)
        stores.append(pltpu.make_async_copy(made.at[part], out.at[part], sems.at[i]))
        stores[-1].start()
    for store in stores:
        store.wait()


def sum_kernel(came, out):
    out[...] = f32_sum([came[j] for j in range(came.shape[0])]).astype(BF16)


def swapped(value, d):
    return lax.ppermute(value, "phon", [(i, i ^ d) for i in range(lax.axis_size("phon"))])


def f32_sum(parts):
    total = parts[0].astype(F32)
    for part in parts[1:]:
        total = total + part.astype(F32)
    return total


def step(queries, keys, values, band_first, cotangent):
    rows, width = queries.shape
    own = keys.shape[0]
    phon = lax.axis_index("phon")
    core = lax.axis_index("frames") & 1
    n = lax.axis_size("frames")
    block = own * n
    half = block // 2
    ranks = lax.axis_size("phon")
    quarter = rows // ranks
    dma = pltpu.SemaphoreType.DMA
    near = [pltpu.VMEM((rows, width), BF16)] * 2

    both = jnp.concatenate([keys, values], axis=1).astype(F32) * LIFT
    every = lax.all_gather(both.astype(jnp.float16), "frames", axis=0, tiled=True)
    every = (every.astype(F32) * (1.0 / LIFT)).astype(BF16)
    tiles = phon * (block // TILE) + jnp.arange(block // TILE, dtype=jnp.int32)
    flags = ((tiles >= band_first[0]) & (tiles < band_first[0] + NBAND)).astype(jnp.int32)
    work = 2 * block * rows * width
    features, stats = call(
        forward_kernel,
        [((rows, width), BF16, HBM), ((3, rows), F32, VMEM)],
        [(flags, SMEM), (every, VMEM), (queries, VMEM), (cotangent, HBM)],
        [
            pltpu.VMEM((block, rows), F32),
            pltpu.VMEM((block, rows), BF16),
            near[0],
            pltpu.VMEM((rows, width), BF16),
            dma((3,)),
        ],
        2 * work,
    )
    heard = [(stats, VMEM), (swapped(stats, 1), VMEM), (swapped(stats, 3), VMEM)]

    def backward(side, space=HBM):
        return call(
            backward_kernel,
            [((half, 2 * width), BF16, space), ((half, rows), BF16, HBM)],
            [
                (jnp.reshape(side, (1,)).astype(jnp.int32), SMEM),
                (flags, SMEM),
                *heard,
                (every, VMEM),
                (queries, VMEM),
                (cotangent, HBM),
            ],
            near[1:]
            + [pltpu.VMEM((half, rows), BF16), dma((5,))]
            + [pltpu.VMEM((half, 2 * width), BF16)] * (space == HBM),
            2 * work,
        )

    send, send_ds = backward(1 - core)
    came = lax.ppermute(send, "frames", [(i, i ^ 1) for i in range(n)])
    keep, keep_ds = backward(core, VMEM)
    (first,) = call(
        add_kernel,
        [((half, 2 * width), BF16, HBM)],
        [(keep, VMEM), (came, VMEM)],
        [pltpu.VMEM((half, 2 * width), BF16), dma((4,))],
    )
    first = lax.all_to_all(
        first.reshape(4, half // 4, 2 * width), "frames", 0, 0, tiled=True,
        axis_index_groups=QUADS,
    )

    place = jnp.stack([phon, core]).astype(jnp.int32)
    parts = call(
        outputs_kernel,
        [((quarter, 2 * width), BF16, VMEM)] * 4,
        [
            (place, SMEM),
            *heard,
            (every, VMEM),
            (features, HBM),
            (keep_ds, HBM),
            (send_ds, HBM),
        ],
        [
            pltpu.VMEM((rows, width), BF16),
            pltpu.VMEM((2, half, rows), BF16),
            pltpu.VMEM((rows, 2 * width), BF16),
            dma((3,)),
        ],
        work,
    )
    moved = [parts[0]] + [swapped(parts[d], d) for d in (2, 1, 3)]

    (second,) = call(sum_kernel, [((half // 4, 2 * width), BF16, VMEM)], [(first, VMEM)])
    second = lax.all_to_all(
        second.reshape(4, own, 2 * width), "frames", 0, 0, tiled=True,
        axis_index_groups=CROSSES,
    )
    mine = f32_sum(moved).astype(BF16)
    spread = [mine] + [swapped(mine, d) for d in (2, 3, 1)]

    def placed(parts):
        whole = jnp.zeros((ranks, quarter, width), BF16)
        for d, p in zip((0, 2, 3, 1), parts):
            whole = lax.dynamic_update_index_in_dim(whole, p, phon ^ d, 0)
        return whole.reshape(rows, width)

    grad_query = placed([m[:, :width] for m in spread])
    aligned = placed([m[:, width:] for m in spread])
    grad = f32_sum([second[i] for i in range(4)])
    return (aligned, grad_query, grad[:, :width], grad[:, width:])


def solution(mesh):
    in_specs = (
        P(("chap", "frames"), None),
        P(("chap", "phon", "frames"), None),
        P(("chap", "phon", "frames"), None),
        P(("chap", "frames")),
        P(("chap", "frames"), None),
    )
    out_specs = (
        P(("chap", "frames"), None),
        P(("chap", "frames"), None),
        P(("chap", "phon", "frames"), None),
        P(("chap", "phon", "frames"), None),
    )
    return jax.shard_map(step, mesh=mesh, in_specs=in_specs, out_specs=out_specs, check_vma=False)
```

```python
import jax
import jax.numpy as jnp
import numpy as np
from jax import lax
from jax.experimental import pallas as pl
from jax.experimental.pallas import tpu as pltpu
from jax.sharding import PartitionSpec as P


TILE = 512
NBAND = 2
NEG_FILL = -1e30
FLOOR = -1e29
LIFT = 4096.0
NT = (((1,), (1,)), ((), ()))
TN = (((0,), (0,)), ((), ()))
F32, BF16 = jnp.float32, jnp.bfloat16


def chip_order(offset):
    return [[(4 * g + (k + g) % 4 + offset) % 16 for g in range(4)] for k in range(4)]


ORDERS = [chip_order(0), chip_order(2)]
QUADS = [[2 * ORDERS[c][k][g] + c for k in range(4)] for c in range(2) for g in range(4)]
CROSSES = [[2 * ORDERS[c][k][g] + c for g in range(4)] for c in range(2) for k in range(4)]
BLOCKS = [2 * ORDERS[c][k][g] + c for c in range(2) for k in range(4) for g in range(4)]


VMEM, HBM, SMEM = pltpu.VMEM, pltpu.HBM, pltpu.SMEM


def call(kernel, outs, args, scratch=(), flops=0):
    shapes = [
        HBM(shape, dtype) if space == HBM else jax.ShapeDtypeStruct(shape, dtype)
        for shape, dtype, space in outs
    ]
    size = sum(a.size * a.dtype.itemsize for a, _ in args)
    size += sum(int(np.prod(o.shape)) * o.dtype.itemsize for o in shapes)
    return pl.pallas_call(
        kernel,
        out_shape=shapes,
        in_specs=[pl.BlockSpec(memory_space=space) for _, space in args],
        out_specs=[pl.BlockSpec(memory_space=space) for _, _, space in outs],
        scratch_shapes=list(scratch),
        cost_estimate=pl.CostEstimate(flops=flops, bytes_accessed=size, transcendentals=0),
        compiler_params=pltpu.CompilerParams(vmem_limit_bytes=16 << 20),
    )(*[pltpu.with_memory_space_constraint(a, HBM) if space == HBM else a for a, space in args])


def half_rows(every, core, own, columns):
    count = len(BLOCKS) // 2
    rows = []
    for i in range(count):
        at = ((BLOCKS[i] + 4 * core) & (2 * count - 1)) + core
        rows.append(every[pl.ds(pl.multiple_of(at * own, own), own), columns])
    return jnp.concatenate(rows, axis=0)


def masked_half(scores, flags, core, own):
    count = len(BLOCKS) // 2
    parts = []
    for i in range(count):
        at = ((BLOCKS[i] + 4 * core) & (2 * count - 1)) + core
        parts.append(
            jnp.where(flags[at * own // TILE] > 0, scores[own * i : own * (i + 1)], NEG_FILL)
        )
    return jnp.concatenate(parts, axis=0)


def forward_kernel(
    flags, every, queries, cotangent_far, features_far, stats,
    scores_at, expd, cotangent, features, sems,
):
    block = every.shape[0]
    rows, width = queries.shape
    scale = width ** (-0.5)
    fetch_g = pltpu.make_async_copy(cotangent_far, cotangent, sems.at[0])
    fetch_g.start()
    peak = jnp.full((1, rows), FLOOR, F32)
    for tile in range(block // TILE):
        here = slice(tile * TILE, (tile + 1) * TILE)
        low_key = every[here, :width]
        key = low_key.astype(F32)
        offset = jnp.sum(key * key, axis=1, keepdims=True) * (-0.5 * scale)
        raw = lax.dot_general(low_key, queries[...], NT, preferred_element_type=F32)
        scores = jnp.where(flags[tile] > 0, raw * scale + offset, NEG_FILL)
        scores_at[here, :] = scores
        peak = jnp.maximum(peak, jnp.max(scores, axis=0, keepdims=True))
    total = jnp.zeros_like(peak)
    for tile in range(block // TILE):
        here = slice(tile * TILE, (tile + 1) * TILE)
        e = jnp.exp(scores_at[here, :] - peak)
        expd[here, :] = e.astype(BF16)
        total += jnp.sum(e, axis=0, keepdims=True)
    deltas, stores = [], []
    for i in range(2):
        part = pl.ds(i * rows // 2, rows // 2)
        out = lax.dot_general(expd[:, part], every[:, width:], TN, preferred_element_type=F32)
        features[part, :] = out.astype(BF16)
        copy = pltpu.make_async_copy(features.at[part], features_far.at[part], sems.at[1 + i])
        copy.start()
        stores.append(copy)
        if i == 0:
            fetch_g.wait()
        delta = jnp.sum(cotangent[part, :].astype(F32) * out, axis=1, keepdims=True)
        deltas.append(jnp.transpose(jnp.broadcast_to(delta, (rows // 2, 128)))[0:1, :])
    delta = jnp.concatenate(deltas, axis=1)
    stats[0:1, :] = peak
    stats[1:2, :] = total
    stats[2:3, :] = delta
    for copy in stores:
        copy.wait()


def merged(heard):
    peaks = [stats[0:1, :] for stats in heard]
    peak = peaks[0]
    for p in peaks[1:]:
        peak = jnp.maximum(peak, p)
    weights = [jnp.exp(p - peak) for p in peaks]
    total = sum(w * stats[1:2, :] for w, stats in zip(weights, heard))
    delta = sum(w * stats[2:3, :] for w, stats in zip(weights, heard))
    return peak, jnp.maximum(total, 0.5), delta


def backward_kernel(
    side, flags, stats, stats_up, stats_down, every, queries, cotangent_far,
    grads_out, ds_far, cotangent, ds_low, sems, *room,
):
    grads = room[0] if room else grads_out
    width = queries.shape[1]
    scale = width ** (-0.5)
    own = every.shape[0] // len(BLOCKS)
    core = side[0]
    fetch_g = pltpu.make_async_copy(cotangent_far, cotangent, sems.at[1])
    fetch_g.start()
    peak, total, delta = merged((stats, stats_up, stats_down))
    delta = delta / total
    lse = peak + jnp.log(total)
    low_key = half_rows(every, core, own, slice(0, width))
    key = low_key.astype(F32)
    offset = jnp.sum(key * key, axis=1, keepdims=True) * (-0.5 * scale)
    raw = lax.dot_general(low_key, queries[...], NT, preferred_element_type=F32)
    fetch_g.wait()
    low_value = half_rows(every, core, own, slice(width, 2 * width))
    dp = lax.dot_general(low_value, cotangent[...], NT, preferred_element_type=F32)
    scores = masked_half(raw * scale + offset, flags, core, own)
    probs = jnp.exp(scores - lse)
    value = jnp.dot(probs.astype(BF16), cotangent[...], preferred_element_type=F32)
    grads[:, width:] = value.astype(BF16)
    right = pl.ds(width, width)
    stores = []
    if room:
        stores += [pltpu.make_async_copy(grads.at[:, right], grads_out.at[:, right], sems.at[4])]
        stores[-1].start()
    ds = probs * (dp - delta)
    low = ds.astype(BF16)
    ds_low[...] = low
    stores += [pltpu.make_async_copy(ds_low, ds_far, sems.at[2])]
    stores[-1].start()
    column = jnp.sum(ds, axis=1, keepdims=True)
    grad = jnp.dot(low, queries[...], preferred_element_type=F32)
    grads[:, :width] = ((grad - column * low_key.astype(F32)) * scale).astype(BF16)
    left = pl.ds(0, width)
    if room:
        stores += [pltpu.make_async_copy(grads.at[:, left], grads_out.at[:, left], sems.at[3])]
        stores[-1].start()
    for store in stores:
        store.wait()


def outputs_kernel(
    place, stats, stats_up, stats_down, every, features_far, keep_far, send_far, *rest
):
    parts, (features, low, gathered, sems) = rest[:4], rest[4:]
    quarter = parts[0].shape[0]
    rows, width = features.shape
    own = every.shape[0] // len(BLOCKS)
    fetches = [
        pltpu.make_async_copy(far, near, sems.at[i])
        for i, (far, near) in enumerate(
            ((features_far, features), (keep_far, low.at[0]), (send_far, low.at[1]))
        )
    ]
    for f in fetches:
        f.start()
    peak, total, _ = merged((stats, stats_up, stats_down))
    share = jnp.exp(stats[0:1, :] - peak) / total
    share = jnp.transpose(jnp.broadcast_to(share, (128, rows)))
    share = jnp.concatenate([share] * (width // 128), axis=1)
    fetches[0].wait()
    gathered[:, width:] = (features[...].astype(F32) * share).astype(BF16)
    query = jnp.zeros((rows, width), F32)
    for i, core in enumerate((place[1], 1 - place[1])):
        fetches[i + 1].wait()
        right = half_rows(every, core, own, slice(0, width))
        query += lax.dot_general(low[i], right, TN, preferred_element_type=F32)
    gathered[:, :width] = (query * width ** (-0.5)).astype(BF16)
    for d, part in enumerate(parts):
        at = (place[0] ^ d) * quarter
        part[...] = gathered[pl.ds(pl.multiple_of(at, quarter), quarter), :]


def add_kernel(keep, came, out, made, sems):
    n = sems.shape[0]
    size = keep.shape[0] // n
    stores = []
    for i in range(n):
        part = pl.ds(size * i, size)
        made[part, :] = (keep[part, :].astype(F32) + came[part, :].astype(F32)).astype(BF16)
        stores.append(pltpu.make_async_copy(made.at[part], out.at[part], sems.at[i]))
        stores[-1].start()
    for store in stores:
        store.wait()


def sum_kernel(came, out):
    out[...] = f32_sum([came[j] for j in range(came.shape[0])]).astype(BF16)


def swapped(value, d):
    return lax.ppermute(value, "phon", [(i, i ^ d) for i in range(lax.axis_size("phon"))])


def f32_sum(parts):
    total = parts[0].astype(F32)
    for part in parts[1:]:
        total = total + part.astype(F32)
    return total


def step(queries, keys, values, band_first, cotangent):
    rows, width = queries.shape
    own = keys.shape[0]
    phon = lax.axis_index("phon")
    core = lax.axis_index("frames") & 1
    n = lax.axis_size("frames")
    block = own * n
    half = block // 2
    ranks = lax.axis_size("phon")
    quarter = rows // ranks
    dma = pltpu.SemaphoreType.DMA
    near = [pltpu.VMEM((rows, width), BF16)] * 2

    both = jnp.concatenate([keys, values], axis=1).astype(F32) * LIFT
    every = lax.all_gather(both.astype(jnp.float16), "frames", axis=0, tiled=True)
    every = (every.astype(F32) * (1.0 / LIFT)).astype(BF16)
    tiles = phon * (block // TILE) + jnp.arange(block // TILE, dtype=jnp.int32)
    flags = ((tiles >= band_first[0]) & (tiles < band_first[0] + NBAND)).astype(jnp.int32)
    work = 2 * block * rows * width
    features, stats = call(
        forward_kernel,
        [((rows, width), BF16, HBM), ((3, rows), F32, VMEM)],
        [(flags, SMEM), (every, VMEM), (queries, VMEM), (cotangent, HBM)],
        [
            pltpu.VMEM((block, rows), F32),
            pltpu.VMEM((block, rows), BF16),
            near[0],
            pltpu.VMEM((rows, width), BF16),
            dma((3,)),
        ],
        2 * work,
    )
    n_phon = lax.axis_size("phon")
    passed = [
        lax.ppermute(stats, "phon", [(i, (i + d) % n_phon) for i in range(n_phon)])
        for d in (1, n_phon - 1)
    ]
    heard = [(stats, VMEM)] + [(p, VMEM) for p in passed]

    def backward(side, space=HBM):
        return call(
            backward_kernel,
            [((half, 2 * width), BF16, space), ((half, rows), BF16, HBM)],
            [
                (jnp.reshape(side, (1,)).astype(jnp.int32), SMEM),
                (flags, SMEM),
                *heard,
                (every, VMEM),
                (queries, VMEM),
                (cotangent, HBM),
            ],
            near[1:]
            + [pltpu.VMEM((half, rows), BF16), dma((5,))]
            + [pltpu.VMEM((half, 2 * width), BF16)] * (space == HBM),
            2 * work,
        )

    send, send_ds = backward(1 - core)
    came = lax.ppermute(send, "frames", [(i, i ^ 1) for i in range(n)])
    keep, keep_ds = backward(core, VMEM)
    (first,) = call(
        add_kernel,
        [((half, 2 * width), BF16, HBM)],
        [(keep, VMEM), (came, VMEM)],
        [pltpu.VMEM((half, 2 * width), BF16), dma((4,))],
    )
    first = lax.all_to_all(
        first.reshape(4, half // 4, 2 * width), "frames", 0, 0, tiled=True,
        axis_index_groups=QUADS,
    )

    place = jnp.stack([phon, core]).astype(jnp.int32)
    parts = call(
        outputs_kernel,
        [((quarter, 2 * width), BF16, VMEM)] * 4,
        [
            (place, SMEM),
            *heard,
            (every, VMEM),
            (features, HBM),
            (keep_ds, HBM),
            (send_ds, HBM),
        ],
        [
            pltpu.VMEM((rows, width), BF16),
            pltpu.VMEM((2, half, rows), BF16),
            pltpu.VMEM((rows, 2 * width), BF16),
            dma((3,)),
        ],
        work,
    )
    moved = [parts[0]] + [swapped(parts[d], d) for d in (2, 1, 3)]

    (second,) = call(sum_kernel, [((half // 4, 2 * width), BF16, VMEM)], [(first, VMEM)])
    second = lax.all_to_all(
        second.reshape(4, own, 2 * width), "frames", 0, 0, tiled=True,
        axis_index_groups=CROSSES,
    )
    mine = f32_sum(moved).astype(BF16)
    spread = [mine] + [swapped(mine, d) for d in (2, 3, 1)]

    def placed(parts):
        whole = jnp.zeros((ranks, quarter, width), BF16)
        for d, p in zip((0, 2, 3, 1), parts):
            whole = lax.dynamic_update_index_in_dim(whole, p, phon ^ d, 0)
        return whole.reshape(rows, width)

    grad_query = placed([m[:, :width] for m in spread])
    aligned = placed([m[:, width:] for m in spread])
    grad = f32_sum([second[i] for i in range(4)])
    return (aligned, grad_query, grad[:, :width], grad[:, width:])


def solution(mesh):
    in_specs = (
        P(("chap", "frames"), None),
        P(("chap", "phon", "frames"), None),
        P(("chap", "phon", "frames"), None),
        P(("chap", "frames")),
        P(("chap", "frames"), None),
    )
    out_specs = (
        P(("chap", "frames"), None),
        P(("chap", "frames"), None),
        P(("chap", "phon", "frames"), None),
        P(("chap", "phon", "frames"), None),
    )
    return jax.shard_map(step, mesh=mesh, in_specs=in_specs, out_specs=out_specs, check_vma=False)
```
